128 devices in a mesh: seq: 16 (over z, y), exp: 8 (over x, core).
Axes of the slice: x: 4, y: 4, z: 4, core: 2. Of those that a mesh axis runs over, the one named last changes fastest.
Arguments:
- scan_input: bfloat16 [16384, 4096], P('seq', 'exp'), may hold values from -6 to 6
- gate_input: bfloat16 [16384, 4096], P('seq', 'exp'), may hold values from -8 to 8
- input_mix: bfloat16 [8, 16, 16384], P('exp', None, 'seq'), may hold values from -3 to 3
- output_mix: bfloat16 [8, 16, 16384], P('exp', None, 'seq'), may hold values from -3 to 3
- step_size: float32 [64, 16384], P('exp', 'seq'), may hold values from 0.025 to 0.1
- decay_rate: float32 [64], P('exp'), may hold values from 0 to 1
- skip_scale: float32 [64], P('exp'), may hold values from 0.5 to 2
- norm_gain: float32 [4096], P('exp'), may hold values from 0.5 to 1.5
- entry_state: float32 [16, 64, 64, 16], P('seq', 'exp'), may hold values from -12 to 12
- out_weight: bfloat16 [4096, 2048], P('exp'), may hold values from -0.09375 to 0.09375
- block_mid: bfloat16 [16384, 2048], P(('seq', 'exp')), may hold values from -6 to 6
- expert_gain: float32 [2048], replicated, may hold values from 0.5 to 1.5
- expert_choice: int32 [16384, 2], P(('seq', 'exp')), may hold values from 0 to 7, all different within a row; in each aligned block of 128 rows (0 to 127, 128 to 255, ...) at most 64 rows name the same one
- route_weight: float32 [16384, 2], P(('seq', 'exp')), may hold values from 0.2 to 0.8
- gate_proj: bfloat16 [8, 2048, 1024], P('exp'), may hold values from -0.125 to 0.125
- up_proj: bfloat16 [8, 2048, 1024], P('exp'), may hold values from -0.125 to 0.125
- down_proj: bfloat16 [8, 1024, 2048], P('exp'), may hold values from -0.1875 to 0.1875
- out_grad: bfloat16 [16384, 2048], P(('seq', 'exp')), may hold values from -6 to 6
Outputs:
- mid_grad: bfloat16 [16384, 2048], P(('seq', 'exp'))
- scan_input_grad: bfloat16 [16384, 4096], P('seq', 'exp')
- gate_input_grad: bfloat16 [16384, 4096], P('seq', 'exp')
- input_mix_grad: float32 [8, 16, 16384], P('exp', None, 'seq')
- output_mix_grad: float32 [8, 16, 16384], P('exp', None, 'seq')
- step_size_grad: float32 [64, 16384], P('exp', 'seq')
- out_weight_grad: float32 [4096, 2048], P('exp', 'seq')
- gate_proj_grad: float32 [8, 2048, 1024], P('exp', 'seq')
- up_proj_grad: float32 [8, 2048, 1024], P('exp', 'seq')
- down_proj_grad: float32 [8, 1024, 2048], P('exp', None, 'seq')
The draws below stay inside these ranges and needn't reach their ends.
Inputs may be any that keep to these rules, and one draw needn't show every extreme that they name: `expert_choice`: each row names two different experts. In the 128 rows of one device no expert is named by more than 64 rows, and in some device's rows one expert is named by exactly 64.
All inputs are finite; a program needn't handle non-finite values.
Results may differ from the reference program's by a relative error of at most 0.013.
Values may be sent and summed in bfloat16 or wider, within the bound.
No kernel may reach another device: no remote copies, remote signals or barrier semaphores. Data moves between devices by JAX's collectives and lax.ppermute only.
A program may use at most 192 MiB of HBM per device.

```python
import math
import jax
import jax.numpy as jnp
import numpy as np
from jax import lax

D = 2048
HEADS = 64
HEAD_DIM = 64
STATE = 16
GROUPS = 8
FF = 1024
BLOCK = 256
TOK_DEV = 128
INNER = 4096
EXPERTS = 8
CAP = 64
SHARD_LEN = 1024
SEQ_LEN = 16384
SHARDS = 16
N_SEQ = 16
N_EXP = 8


def draw_decay_rate(key, part):
    pick_key, slow_key, fast_key = jax.random.split(key, 3)
    slow_share = 0.5
    slow_rate = jax.random.uniform(slow_key, (HEADS,), jnp.float32, 8.0, 24.0) / SEQ_LEN
    fast_rate = jax.random.uniform(fast_key, (HEADS,), jnp.float32, 0.3, 0.6)
    chosen = jax.random.bernoulli(pick_key, slow_share, (HEADS,))
    return jnp.where(chosen, slow_rate, fast_rate).astype(jnp.float32)


def shard_levels(stream_key, shape, cuts, low, top_value):
    gain = 1.0
    for position, parts in cuts:
        heights = jax.random.uniform(jax.random.fold_in(jax.random.fold_in(stream_key, 6), position), (parts,), jnp.float32, low / len(cuts), top_value / len(cuts))
        gain = gain * jnp.repeat(jnp.exp(heights), shape[position] // parts).reshape((-1,) + (1,) * (len(shape) - 1 - position))
    return gain


def deal_out(rng, own, number, rows, number_of, top, limit, slope):
    sequence = jax.random.permutation(rng, number_of)
    packed, usual = load_shares(number_of, rows * top, limit, slope, True), load_shares(number_of, rows * top, limit, slope, False)
    places = jnp.arange(number_of)

    def named(lengths, offset_by):
        used = int((lengths > 0).sum())
        fixed = max(1, used // 4)
        shifted = fixed + (places - fixed + offset_by * (used - fixed)) % max(1, number_of - fixed)
        return jnp.zeros((number_of,), jnp.int32).at[sequence[jnp.where(places < fixed, places, shifted)]].set(jnp.asarray(lengths, jnp.int32))

    lengths = jnp.where(number % 4 == 0, named(packed, number // 4), named(usual, number - number // 4 - 1))
    mixed = jax.random.permutation(jax.random.fold_in(own, 3), number_of)
    donor, receiver = mixed[0:number_of // 2 * 2:2], mixed[1:number_of // 2 * 2:2]
    margin = jnp.minimum(lengths[donor] - 1, limit - lengths[receiver]) // 2
    margin = jnp.where((donor == sequence[0]) | (receiver == sequence[0]) | (lengths[receiver] == 0), 0, jnp.maximum(margin, 0))
    shifted = jax.random.randint(jax.random.fold_in(own, 4), (number_of // 2,), 0, 1 << 20) % (margin + 1)
    lengths = lengths.at[donor].add(-shifted).at[receiver].add(shifted)
    labels = jnp.searchsorted(jnp.cumsum(lengths), jnp.arange(rows * top), side="right").astype(jnp.int32)
    listing = labels.reshape(top, rows).T
    listing = listing[jax.random.permutation(jax.random.fold_in(own, 1), rows)]
    offset_by = jax.random.randint(jax.random.fold_in(own, 2), (rows, 1), 0, top)
    return jnp.take_along_axis(listing, (jnp.arange(top)[None, :] + offset_by) % top, axis=1)


def load_shares(number_of, total, most, skew, full):
    weights = [(1 << 20) // math.isqrt(standing ** skew) + 1 for standing in range(1, number_of + 1)]
    largest = most if full else min(most, max(-(-total // number_of), total * weights[0] // sum(weights)))
    least = 1 if total - largest >= number_of - 1 else 0
    counts, rest = [largest] + [least] * (number_of - 1), total - largest - least * (number_of - 1)
    while rest > 0:
        movable = [i for i in range(1, number_of) if counts[i] < largest] or [i for i in range(1, number_of) if counts[i] < most]
        pool, remaining = sum([weights[i] for i in movable]), rest
        for i in movable:
            extra = min(most - counts[i], max(1, remaining * weights[i] // pool), rest)
            counts[i] = counts[i] + extra
            rest = rest - extra
    return np.array(counts)


def scatter_about(own_key, extent, deviation, bound, cuts=(), kind=jnp.bfloat16):
    result = deviation * jax.random.normal(own_key, extent, jnp.float32)
    if cuts:
        result = result * shard_levels(own_key, extent, cuts, -0.22, 0.18)
    return jnp.clip(result, -bound, bound).astype(kind)


def setup_inputs(seed: int = 0) -> dict:
    key_list = jax.random.split(jax.random.key(seed), 19)
    scan_input = scatter_about(key_list[0], (SEQ_LEN, INNER), 1.0, 6.0, ((0, 16), (1, 8)))
    gate_input = scatter_about(key_list[1], (SEQ_LEN, INNER), 1.5, 8.0, ((0, 16), (1, 8)))
    input_mix = scatter_about(key_list[2], (GROUPS, STATE, SEQ_LEN), 0.5, 3.0, ((0, 8), (2, 16)))
    output_mix = scatter_about(key_list[3], (GROUPS, STATE, SEQ_LEN), 0.5, 3.0, ((0, 8), (2, 16)))
    step_size = jnp.clip(jnp.exp(math.log(0.1) - 1.3862944 * jax.random.uniform(key_list[4], (HEADS, SEQ_LEN), jnp.float32) ** shard_levels(key_list[4], (HEADS, SEQ_LEN), ((0, 8), (1, 16)), -0.2, 0.2)), 0.025, 0.1)
    decay_rate = draw_decay_rate(jax.random.fold_in(key_list[18], 71), 0)
    skip_scale = jnp.clip(0.5 + 1.5 * jax.random.uniform(key_list[6], (HEADS,), jnp.float32) ** shard_levels(key_list[6], (HEADS,), ((0, 8),), -0.2, 0.2), 0.5, 2.0)
    norm_gain = jnp.clip(1.0 + 0.1 * jax.random.normal(key_list[7], (INNER,), jnp.float32), 0.5, 1.5)
    entry_state = scatter_about(key_list[8], (SHARDS, HEADS, HEAD_DIM, STATE), 2.0, 12.0, ((0, 16), (1, 8)), jnp.float32)
    out_weight = scatter_about(key_list[9], (INNER, D), INNER ** -0.5, 0.09375, ((0, 8),))
    block_mid = scatter_about(key_list[10], (SEQ_LEN, D), 1.0, 6.0, ((0, 128),))
    expert_gain = jnp.clip(1.0 + 0.1 * jax.random.normal(key_list[11], (D,), jnp.float32), 0.5, 1.5)
    expert_choice_keys = jax.random.split(jax.random.fold_in(key_list[12], 1), SEQ_LEN // TOK_DEV)
    expert_choice_turns = jax.random.permutation(jax.random.fold_in(key_list[12], 3), SEQ_LEN // TOK_DEV)
    expert_choice = jax.vmap(lambda own, number: deal_out(jax.random.fold_in(key_list[12], 2), own, number, TOK_DEV, EXPERTS, 2, CAP, 2))(expert_choice_keys, expert_choice_turns).reshape((SEQ_LEN, 2))
    route_weight = jnp.clip(0.2 + 0.6 * jax.random.uniform(key_list[13], (SEQ_LEN, 2), jnp.float32) ** shard_levels(key_list[13], (SEQ_LEN, 2), ((0, 128),), -0.2, 0.2), 0.2, 0.8)
    gate_proj = scatter_about(key_list[14], (EXPERTS, D, FF), D ** -0.5, 0.125, ((0, 8),))
    up_proj = scatter_about(key_list[15], (EXPERTS, D, FF), D ** -0.5, 0.125, ((0, 8),))
    down_proj = scatter_about(key_list[16], (EXPERTS, FF, D), FF ** -0.5, 0.1875, ((0, 8),))
    out_grad = scatter_about(key_list[17], (SEQ_LEN, D), 1.0, 6.0, ((0, 128),))
    return {"scan_input": scan_input, "gate_input": gate_input, "input_mix": input_mix, "output_mix": output_mix, "step_size": step_size, "decay_rate": decay_rate, "skip_scale": skip_scale, "norm_gain": norm_gain, "entry_state": entry_state, "out_weight": out_weight, "block_mid": block_mid, "expert_gain": expert_gain, "expert_choice": expert_choice, "route_weight": route_weight, "gate_proj": gate_proj, "up_proj": up_proj, "down_proj": down_proj, "out_grad": out_grad}


norm_eps = 1e-05
highest = lax.Precision.HIGHEST

def silu_parts(values):
    sigmoid = jax.nn.sigmoid(values)
    return (values * sigmoid, sigmoid * (1.0 + values * (1.0 - sigmoid)))

def row_products(left_rows, right_rows):
    return lax.dot_general(left_rows, right_rows, (((0,), (0,)), ((), ())), preferred_element_type=jnp.float32)

def expert_core(rows_in, rows_grad, gate_matrix, up_matrix, down_matrix):
    contract_cols = (((1,), (1,)), ((), ()))
    gate_pre = jnp.dot(rows_in, gate_matrix, preferred_element_type=jnp.float32)
    up_pre = jnp.dot(rows_in, up_matrix, preferred_element_type=jnp.float32)
    gate_act, gate_slope = silu_parts(gate_pre)
    hidden = (gate_act * up_pre).astype(jnp.bfloat16)
    hidden_back = lax.dot_general(rows_grad, down_matrix, contract_cols, preferred_element_type=jnp.float32)
    gate_back = (hidden_back * up_pre * gate_slope).astype(jnp.bfloat16)
    up_back = (hidden_back * gate_act).astype(jnp.bfloat16)
    rows_back = lax.dot_general(gate_back, gate_matrix, contract_cols, preferred_element_type=jnp.float32)
    rows_back = rows_back + lax.dot_general(up_back, up_matrix, contract_cols, preferred_element_type=jnp.float32)
    return (rows_back.astype(jnp.bfloat16), hidden, gate_back, up_back)

def adjoint_blocks(incoming, block_decay, block_adj):

    def retreat(carried, inputs):
        decay_now, adj_now = inputs
        return (adj_now + decay_now[..., None, None] * carried, carried)
    return lax.scan(retreat, incoming, (block_decay, block_adj), reverse=True)

def prepare(scan_input, gate_input, input_mix, output_mix, step_size, decay_rate, skip_scale, norm_gain, entry_state):
    length = scan_input.shape[0]
    head_count = step_size.shape[0]
    groups = input_mix.shape[0]
    states = input_mix.shape[1]
    per_group = head_count // groups
    head_width = scan_input.shape[1] // head_count
    blocks = length // BLOCK
    signal = scan_input.astype(jnp.float32).reshape(blocks, BLOCK, groups, per_group, head_width)
    gating = gate_input.astype(jnp.float32).reshape(blocks, BLOCK, groups, per_group, head_width)
    mix_in = input_mix.astype(jnp.float32).reshape(groups, states, blocks, BLOCK).transpose(2, 0, 1, 3)
    mix_out = output_mix.astype(jnp.float32).reshape(groups, states, blocks, BLOCK).transpose(2, 0, 1, 3)
    head_rates = -decay_rate.reshape(groups, per_group)
    step_blk = step_size.reshape(groups, per_group, blocks, BLOCK).transpose(2, 0, 1, 3)
    log_cum = jnp.cumsum(step_blk * head_rates[None, :, :, None], axis=3)
    positions = jnp.arange(BLOCK, dtype=jnp.int32)
    lower_tri = positions[:, None] >= positions[None, :]
    log_gaps = log_cum[..., :, None] - log_cum[..., None, :]
    decay_mask = jnp.where(lower_tri, jnp.exp(jnp.where(lower_tri, log_gaps, 0.0)), 0.0)
    mix_dot = jnp.einsum('bgni,bgnj->bgij', mix_out, mix_in, precision=highest)
    forward_kernel = decay_mask * mix_dot[:, :, None] * step_blk[:, :, :, None, :]
    inside = jnp.einsum('bghij,bjghp->bighp', forward_kernel, signal, precision=highest)
    end_weight = jnp.exp(log_cum[..., -1:] - log_cum) * step_blk
    block_state = jnp.einsum('bghj,bjghp,bgnj->bghpn', end_weight, signal, mix_in, precision=highest)
    block_decay = jnp.exp(log_cum[..., -1])
    start_state = entry_state.reshape(groups, per_group, head_width, states).astype(jnp.float32)

    def advance(carried, inputs):
        decay_now, state_now = inputs
        return (decay_now[..., None, None] * carried + state_now, carried)
    _, begin_states = lax.scan(advance, start_state, (block_decay, block_state))
    from_state = jnp.einsum('bghpn,bgni->bighp', begin_states, mix_out, precision=highest)
    from_state = from_state * jnp.exp(log_cum).transpose(0, 3, 1, 2)[..., None]
    skip_vals = skip_scale.reshape(groups, per_group)
    output = inside + from_state + skip_vals[:, :, None] * signal
    gate_act, gate_slope = silu_parts(gating)
    gated = output * gate_act
    gain_vals = norm_gain.reshape(groups, per_group, head_width)
    group_scale = lax.rsqrt(lax.optimization_barrier(jnp.mean(gated * gated, axis=(3, 4), keepdims=True)) + norm_eps)
    normed = (gated * group_scale * gain_vals).astype(jnp.bfloat16).reshape(length, head_count * head_width)
    context = (signal, mix_in, mix_out, step_blk, log_cum, head_rates, decay_mask, mix_dot, begin_states, from_state, output, gated, group_scale, gain_vals, skip_vals, gate_act, gate_slope, block_decay)
    return (context, normed)

def local_adjoint(context, normed_back):
    signal, mix_in, mix_out, step_blk, log_cum, head_rates, decay_mask, mix_dot, begin_states, from_state, output, gated, group_scale, gain_vals, skip_vals, gate_act, gate_slope, block_decay = context
    scaled_back = normed_back.reshape(signal.shape) * gain_vals
    gated_back = group_scale * scaled_back - gated * group_scale ** 3 * lax.optimization_barrier(jnp.mean(gated * scaled_back, axis=(3, 4), keepdims=True))
    out_back = gated_back * gate_act
    gate_grad = (gated_back * output * gate_slope).astype(jnp.bfloat16).reshape(normed_back.shape)
    block_adj = jnp.einsum('bghi,bighp,bgni->bghpn', jnp.exp(log_cum), out_back, mix_out, precision=highest)
    shard_adj, _ = adjoint_blocks(jnp.zeros_like(block_adj[0]), block_decay, block_adj)
    shard_decay = jnp.exp(lax.optimization_barrier(jnp.sum(log_cum[..., -1], axis=0)))
    return (out_back, gate_grad, shard_adj, shard_decay, block_adj)

def finish_grads(context, out_back, block_adj, incoming):
    signal, mix_in, mix_out, step_blk, log_cum, head_rates, decay_mask, mix_dot, begin_states, from_state, output, gated, group_scale, gain_vals, skip_vals, gate_act, gate_slope, block_decay = context
    blocks, block_len, groups, per_group, head_width = signal.shape
    states = mix_in.shape[2]
    _, end_adj = adjoint_blocks(incoming, block_decay, block_adj)
    positions = jnp.arange(BLOCK, dtype=jnp.int32)
    before = (positions[:, None] < positions[None, :]).astype(jnp.float32)
    not_after = (positions[:, None] >= positions[None, :]).astype(jnp.float32)
    pair_dot = jnp.einsum('bighp,bjghp->bghij', out_back, signal, precision=highest)
    weighted = decay_mask * step_blk[:, :, :, None, :] * pair_dot
    group_pair = lax.optimization_barrier(jnp.sum(weighted, axis=2))
    end_decay = jnp.exp(log_cum[..., -1:] - log_cum)
    end_back = jnp.einsum('bghpn,bgnj->bjghp', end_adj, mix_in, precision=highest)
    end_back = end_back * end_decay.transpose(0, 3, 1, 2)[..., None]
    adjoint_mix = jnp.einsum('bghij,bighp->bjghp', decay_mask * mix_dot[:, :, None], out_back, precision=highest) + end_back
    step_col = step_blk.transpose(0, 3, 1, 2)[..., None]
    input_grad = (skip_vals[:, :, None] * out_back + step_col * adjoint_mix).astype(jnp.bfloat16)
    in_mix_grad = jnp.einsum('bgij,bgni->bgnj', group_pair, mix_out, precision=highest)
    in_mix_grad = in_mix_grad + jnp.einsum('bghj,bghpn,bjghp->bgnj', step_blk * end_decay, end_adj, signal, precision=highest)
    out_mix_grad = jnp.einsum('bgij,bgnj->bgni', group_pair, mix_in, precision=highest)
    out_mix_grad = out_mix_grad + jnp.einsum('bghi,bghpn,bighp->bgni', jnp.exp(log_cum), begin_states, out_back, precision=highest)
    pair_terms = weighted * mix_dot[:, :, None]
    split_sum = jnp.einsum('bghij,jt->bghit', pair_terms, before, precision=highest)
    straddle = lax.optimization_barrier(jnp.sum(split_sum * not_after, axis=3))
    state_term = lax.optimization_barrier(jnp.sum(out_back * from_state, axis=4)).transpose(0, 2, 3, 1)
    state_tail = jnp.einsum('bghi,it->bght', state_term, not_after, precision=highest)
    end_term = step_blk * lax.optimization_barrier(jnp.sum(signal * end_back, axis=4)).transpose(0, 2, 3, 1)
    end_head = jnp.einsum('bghj,jt->bght', end_term, before, precision=highest)
    whole_term = block_decay * lax.optimization_barrier(jnp.sum(end_adj * begin_states, axis=(3, 4)))
    log_grad = straddle + state_tail + end_head + whole_term[..., None]
    step_grad = head_rates[None, :, :, None] * log_grad + lax.optimization_barrier(jnp.sum(signal * adjoint_mix, axis=4)).transpose(0, 2, 3, 1)
    length = blocks * block_len
    input_grad = input_grad.reshape(length, groups * per_group * head_width)
    in_mix_grad = in_mix_grad.transpose(1, 2, 0, 3).reshape(groups, states, length)
    out_mix_grad = out_mix_grad.transpose(1, 2, 0, 3).reshape(groups, states, length)
    step_grad = step_grad.transpose(1, 2, 0, 3).reshape(groups * per_group, length)
    return (input_grad, in_mix_grad, out_mix_grad, step_grad)

def reference(scan_input, gate_input, input_mix, output_mix, step_size, decay_rate, skip_scale, norm_gain, entry_state, out_weight, block_mid, expert_gain, expert_choice, route_weight, gate_proj, up_proj, down_proj, out_grad):
    shards = N_SEQ
    shard_len = SHARD_LEN
    capacity = N_EXP * CAP
    mid_values = block_mid.astype(jnp.float32)
    mid_scale = lax.rsqrt(lax.optimization_barrier(jnp.mean(mid_values * mid_values, axis=1, keepdims=True)) + norm_eps)
    normed_mid = (mid_values * mid_scale * expert_gain).astype(jnp.bfloat16)
    slot_grad = (route_weight[:, :, None] * out_grad.astype(jnp.float32)[:, None, :]).astype(jnp.bfloat16)

    def shard_experts(totals, inputs):
        tokens_in, grads_in, chosen = inputs
        flat_grads = grads_in.reshape(2 * shard_len, D)

        def one_expert(expert):
            expert_hits = chosen == expert
            where_rows = jnp.nonzero(expert_hits, size=capacity, fill_value=0)[0].astype(jnp.int32)
            live_rows = jnp.arange(capacity, dtype=jnp.int32) < jnp.sum(expert_hits.astype(jnp.int32))
            rows_in = jnp.where(live_rows[:, None], tokens_in[where_rows // 2], jnp.zeros((), tokens_in.dtype))
            rows_grad = jnp.where(live_rows[:, None], flat_grads[where_rows], jnp.zeros((), flat_grads.dtype))
            rows_back, hidden, gate_back, up_back = expert_core(rows_in, rows_grad, gate_proj[expert], up_proj[expert], down_proj[expert])
            partials = (row_products(rows_in, gate_back).astype(jnp.bfloat16), row_products(rows_in, up_back).astype(jnp.bfloat16), row_products(rows_grad, hidden).astype(jnp.bfloat16))
            return (rows_back, where_rows, live_rows, partials)
        rows_back, where_rows, live_rows, partials = lax.map(one_expert, jnp.arange(EXPERTS, dtype=jnp.int32))
        back_vals = jnp.where(live_rows[..., None], rows_back.astype(jnp.float32), 0.0).reshape(-1, D)
        slot_sums = jnp.zeros((2 * shard_len, D), jnp.float32).at[where_rows.reshape(-1)].add(back_vals)
        branch_part = slot_sums.reshape(shard_len, 2, D).sum(axis=1)
        totals = tuple((running + partial_value.astype(jnp.float32) for running, partial_value in zip(totals, partials)))
        return (totals, branch_part)
    zero_terms = tuple((jnp.zeros((EXPERTS, D, FF), jnp.float32) for _ in range(3)))
    expert_totals, branch_back = lax.scan(shard_experts, zero_terms, (normed_mid.reshape(shards, shard_len, D), slot_grad.reshape(shards, shard_len, 2, D), expert_choice.reshape(shards, shard_len * 2)))
    branch_back = branch_back.reshape(SEQ_LEN, D)
    weighted_back = branch_back * expert_gain
    mid_grad = (out_grad.astype(jnp.float32) + mid_scale * weighted_back - mid_values * mid_scale ** 3 * lax.optimization_barrier(jnp.mean(mid_values * weighted_back, axis=1, keepdims=True))).astype(jnp.bfloat16)
    scan_split = scan_input.reshape(shards, shard_len, INNER)
    gate_split = gate_input.reshape(shards, shard_len, INNER)
    in_split = input_mix.reshape(GROUPS, STATE, shards, shard_len).transpose(2, 0, 1, 3)
    out_split = output_mix.reshape(GROUPS, STATE, shards, shard_len).transpose(2, 0, 1, 3)
    step_split = step_size.reshape(HEADS, shards, shard_len).transpose(1, 0, 2)
    mid_split = mid_grad.reshape(shards, shard_len, D)
    contract_cols = (((1,), (1,)), ((), ()))

    def local_pass(inputs):
        scan_part, gate_part, in_part, out_part, step_part, entry_part, mid_part = inputs
        context, normed = prepare(scan_part, gate_part, in_part, out_part, step_part, decay_rate, skip_scale, norm_gain, entry_part)
        normed_back = lax.dot_general(mid_part, out_weight, contract_cols, preferred_element_type=jnp.float32)
        return (context, normed, local_adjoint(context, normed_back))

    def first_pass(carried, inputs):
        context, normed, adjoint_parts = local_pass(inputs)
        carried = carried + row_products(inputs[6], normed).astype(jnp.bfloat16).astype(jnp.float32)
        return (carried, (adjoint_parts[2], adjoint_parts[3]))
    stacked = (scan_split, gate_split, in_split, out_split, step_split, entry_state, mid_split)
    weight_total, (shard_adjs, shard_decays) = lax.scan(first_pass, jnp.zeros((D, INNER), jnp.float32), stacked)

    def chain(carried, inputs):
        adj_now, decay_now = inputs
        return (adj_now + decay_now[..., None, None] * carried, carried)
    _, incoming = lax.scan(chain, jnp.zeros_like(shard_adjs[0]), (shard_adjs, shard_decays), reverse=True)

    def second_pass(inputs):
        context, normed, adjoint_parts = local_pass(inputs[:7])
        out_back, gate_grad, shard_adj, shard_decay, block_adj = adjoint_parts
        input_grad, in_mix_grad, out_mix_grad, step_grad = finish_grads(context, out_back, block_adj, inputs[7])
        return (input_grad, gate_grad, in_mix_grad, out_mix_grad, step_grad)
    results = lax.map(second_pass, stacked + (incoming,))
    scan_input_grad = results[0].reshape(SEQ_LEN, INNER)
    gate_input_grad = results[1].reshape(SEQ_LEN, INNER)
    input_mix_grad = results[2].transpose(1, 2, 0, 3).reshape(GROUPS, STATE, SEQ_LEN)
    output_mix_grad = results[3].transpose(1, 2, 0, 3).reshape(GROUPS, STATE, SEQ_LEN)
    step_size_grad = results[4].transpose(1, 0, 2).reshape(HEADS, SEQ_LEN)
    out_weight_grad = weight_total.T
    return (mid_grad, scan_input_grad, gate_input_grad, input_mix_grad, output_mix_grad, step_size_grad, out_weight_grad, expert_totals[0], expert_totals[1], expert_totals[2].transpose(0, 2, 1))
```

```python
import jax
import jax.numpy as jnp
from jax import lax
from jax.experimental import pallas as pl
from jax.experimental.pallas import tpu as pltpu
from jax.sharding import Mesh
from jax.sharding import PartitionSpec as P

BLOCK = 256
EXP = ("exp_0", "exp_1")
SEQ_EXP = ("seq", "exp_0", "exp_1")
norm_eps = 1e-05
highest = lax.Precision.HIGHEST
f32 = jnp.float32
bf16 = jnp.bfloat16


def dot(a, b, dims=((1,), (0,)), precision=None):
    return lax.dot_general(a, b, (dims, ((), ())), preferred_element_type=f32, precision=precision)


NT = ((1,), (1,))
TN = ((0,), (0,))


def split_two(value):
    high = value.astype(bf16)
    return high, (value - high.astype(f32)).astype(bf16)


def head_of_channel(heads, channels):
    row = lax.broadcasted_iota(jnp.int32, (heads, channels), 0)
    col = lax.broadcasted_iota(jnp.int32, (heads, channels), 1)
    return (col // (channels // heads) == row).astype(bf16)


def spread(per_head, owner):
    high, low = split_two(per_head)
    return dot(high, owner, TN) + dot(low, owner, TN)


def head_sums(owner, value):
    high, low = split_two(value)
    return dot(owner, high, NT) + dot(owner, low, NT)


def as_column(row):
    size = row.shape[1]
    same = lax.broadcasted_iota(jnp.int32, (size, size), 0) == lax.broadcasted_iota(jnp.int32, (size, size), 1)
    return jnp.sum(jnp.where(same, row, 0.0), axis=1, keepdims=True)


def limits(mib):
    return pltpu.CompilerParams(vmem_limit_bytes=mib << 20)


def cost(micros):
    return pl.CostEstimate(flops=int(micros * 9e8), transcendentals=0, bytes_accessed=int(micros * 2e6))


def head_row(owner, column):
    return jnp.sum(owner.astype(f32) * column, axis=0, keepdims=True)


def log_cumulative(step, rate):
    tokens = step.shape[1]
    row = lax.broadcasted_iota(jnp.int32, (tokens, tokens), 0)
    col = lax.broadcasted_iota(jnp.int32, (tokens, tokens), 1)
    return dot(-step * rate, (row <= col).astype(f32), precision=highest)


def silu_parts(values):
    sigmoid = 1.0 / (1.0 + jnp.exp(-values))
    return values * sigmoid, sigmoid * (1.0 + values * (1.0 - sigmoid))


def forward_body(x_ref, z_ref, b_ref, c_ref, step_ref, rate_ref, skip_ref, gain_ref, entry_ref,
                 y_ref, normed_ref, begin_ref, state_ref):
    heads, tokens = step_ref.shape
    channels = x_ref.shape[1]
    width = channels // heads

    @pl.when(pl.program_id(0) == 0)
    def _():
        state_ref[...] = entry_ref[...].T

    owner = head_of_channel(heads, channels)
    x = x_ref[...].astype(f32)
    step = step_ref[...]
    log_cum = log_cumulative(step, as_column(rate_ref[...]))
    log_col = log_cum.T
    mix_in, mix_out = b_ref[...], c_ref[...]
    stepped = x * spread(step, owner)
    stepped_bf = stepped.astype(bf16)
    mix_dot = dot(mix_out, mix_in, TN)
    row = lax.broadcasted_iota(jnp.int32, (tokens, tokens), 0)
    col = lax.broadcasted_iota(jnp.int32, (tokens, tokens), 1)
    lower = row >= col
    parts = []
    for h in range(heads):
        gaps = log_col[:, h : h + 1] - log_cum[h : h + 1, :]
        kernel = (jnp.exp(jnp.where(lower, gaps, -1e30)) * mix_dot).astype(bf16)
        parts.append(dot(kernel, stepped_bf[:, h * width : (h + 1) * width]))
    state = state_ref[...]
    begin_ref[...] = state
    from_state = dot(mix_out.astype(f32), state, TN) * spread(jnp.exp(log_cum), owner)
    y = jnp.concatenate(parts, axis=1) + from_state + head_row(owner, as_column(skip_ref[...])) * x
    y_ref[...] = y
    last = log_cum[:, tokens - 1 :]
    ended = (stepped * spread(jnp.exp(last - log_cum), owner)).astype(bf16)
    state_ref[...] = head_row(owner, jnp.exp(last)) * state + dot(mix_in, ended)
    gate_act, _ = silu_parts(z_ref[...].astype(f32))
    gated = y * gate_act
    scale = lax.rsqrt(jnp.mean(gated * gated, axis=1, keepdims=True) + norm_eps)
    normed_ref[...] = (gated * scale * gain_ref[...]).astype(bf16)


def squeezed(*shape):
    return (pl.Squeezed(), *shape)


def scan_forward(x, z, mix_in, mix_out, step, rate, skip, gain, entry):
    length, channels = x.shape
    heads = step.shape[0]
    states = mix_in.shape[1]
    blocks = length // BLOCK
    whole = lambda shape: pl.BlockSpec(shape, lambda b: (0,) * len(shape))
    rows = pl.BlockSpec((BLOCK, channels), lambda b: (b, 0))
    mix = pl.BlockSpec(squeezed(states, BLOCK), lambda b: (0, 0, b))
    return pl.pallas_call(
        forward_body,
        grid=(blocks,),
        in_specs=[rows, rows, mix, mix, pl.BlockSpec((heads, BLOCK), lambda b: (0, b)),
                  whole((1, heads)), whole((1, heads)), whole((1, channels)), whole((channels, states))],
        out_specs=[rows, rows, pl.BlockSpec(squeezed(states, channels), lambda b: (b, 0, 0))],
        out_shape=[jax.ShapeDtypeStruct((length, channels), f32),
                   jax.ShapeDtypeStruct((length, channels), bf16),
                   jax.ShapeDtypeStruct((blocks, states, channels), f32)],
        scratch_shapes=[pltpu.VMEM((states, channels), f32)],
        compiler_params=limits(24),
        cost_estimate=cost(9),
        name="scan_forward",
    )(x, z, mix_in, mix_out, step, rate, skip, gain, entry)


def backward_body(place_ref, *refs):
    pieces = refs[:10]
    (weight_ref, y_ref, z_ref, c_ref, step_ref, rate_ref, gain_ref,
     out_back_ref, gate_grad_ref, end_ref, joined_ref, rows_ref, state_ref, decay_ref, all_ref) = refs[10:]
    heads, tokens = step_ref.shape
    channels = y_ref.shape[1]
    states = state_ref.shape[0]

    @pl.when(pl.program_id(0) == 0)
    def _():
        state_ref[...] = jnp.zeros_like(state_ref)
        decay_ref[...] = jnp.ones_like(decay_ref)
        count = pieces[0].shape[0]
        half = count // 2
        for side in range(2):
            for turn in range(5):
                start = chunk_index(place_ref, side * 4 + min(turn, 3)) * count + (half if turn == 4 else 0)
                piece = pieces[side * 5 + turn]
                all_ref[pl.ds(pl.multiple_of(start, half), piece.shape[0]), :] = piece[...]

    owner = head_of_channel(heads, channels)
    log_cum = log_cumulative(step_ref[...], as_column(rate_ref[...]))
    block = pl.num_programs(0) - 1 - pl.program_id(0)
    rows = all_ref[pl.ds(pl.multiple_of(block * tokens, tokens), tokens), :]
    rows_ref[...] = rows
    projected = dot(rows, weight_ref[...], NT)
    y = y_ref[...]
    gate_act, gate_slope = silu_parts(z_ref[...].astype(f32))
    gated = y * gate_act
    scale = lax.rsqrt(jnp.mean(gated * gated, axis=1, keepdims=True) + norm_eps)
    scaled = projected * gain_ref[...]
    inner = jnp.mean(gated * scaled, axis=1, keepdims=True)
    gated_back = scale * scaled - gated * (scale * scale * scale * inner)
    out_back = gated_back * gate_act
    gate_grad_ref[...] = (gated_back * y * gate_slope).astype(bf16)
    out_back_ref[...] = out_back
    state = state_ref[...]
    end_ref[...] = state
    decayed = (out_back * spread(jnp.exp(log_cum), owner)).astype(bf16)
    block_decay = head_row(owner, jnp.exp(log_cum[:, tokens - 1 :]))
    state = block_decay * state + dot(c_ref[...], decayed)
    decay = block_decay * decay_ref[...]
    state_ref[...] = state
    decay_ref[...] = decay
    joined_ref[:states, :] = state.astype(bf16)
    joined_ref[states:, :] = decay.astype(bf16)


def scan_backward(place, pieces, weight, y, z, mix_out, step, rate, gain):
    length, channels = y.shape
    heads = step.shape[0]
    states = mix_out.shape[1]
    blocks = length // BLOCK
    last = blocks - 1
    width = weight.shape[1]
    whole = lambda shape: pl.BlockSpec(shape, lambda b, place: (0,) * len(shape))
    rows = pl.BlockSpec((BLOCK, channels), lambda b, place: (last - b, 0))
    mix = pl.BlockSpec(squeezed(states, BLOCK), lambda b, place: (0, 0, last - b))
    return pl.pallas_call(
        backward_body,
        grid_spec=pltpu.PrefetchScalarGridSpec(
            num_scalar_prefetch=1,
            grid=(blocks,),
            in_specs=[whole(piece.shape) for piece in pieces] + [
                whole(weight.shape), rows, rows, mix,
                pl.BlockSpec((heads, BLOCK), lambda b, place: (0, last - b)),
                whole((1, heads)), whole((1, channels))],
            out_specs=[rows, rows, pl.BlockSpec(squeezed(states, channels), lambda b, place: (last - b, 0, 0)),
                       whole((states + 1, channels)),
                       pl.BlockSpec((BLOCK, width), lambda b, place: (last - b, 0))],
            scratch_shapes=[pltpu.VMEM((states, channels), f32), pltpu.VMEM((1, channels), f32),
                            pltpu.VMEM((length, width), bf16)],
        ),
        out_shape=[jax.ShapeDtypeStruct((length, channels), f32),
                   jax.ShapeDtypeStruct((length, channels), bf16),
                   jax.ShapeDtypeStruct((blocks, states, channels), f32),
                   jax.ShapeDtypeStruct((states + 1, channels), bf16),
                   jax.ShapeDtypeStruct((length, width), bf16)],
        compiler_params=limits(36),
        cost_estimate=cost(9),
        name="scan_backward",
    )(place, *pieces, weight, y, z, mix_out, step, rate, gain)


def pairs_body(x_ref, ob_ref, b_ref, c_ref, step_ref, rate_ref, begin_ref,
               adj_ref, in_ref, out_ref, log_ref):
    heads, tokens = step_ref.shape
    channels = x_ref.shape[1]
    width = channels // heads
    owner = head_of_channel(heads, channels)
    step = step_ref[...]
    log_cum = log_cumulative(step, as_column(rate_ref[...]))
    log_col = log_cum.T
    mix_in, mix_out = b_ref[...], c_ref[...]
    out_back = ob_ref[...]
    out_back_bf = out_back.astype(bf16)
    stepped = (x_ref[...].astype(f32) * spread(step, owner)).astype(bf16)
    mix_dot = dot(mix_in, mix_out, TN)
    row = lax.broadcasted_iota(jnp.int32, (tokens, tokens), 0)
    col = lax.broadcasted_iota(jnp.int32, (tokens, tokens), 1)
    upper = row <= col
    group_pair = jnp.zeros((tokens, tokens), f32)
    parts, later, earlier = [], [], []
    for h in range(heads):
        gaps = log_cum[h : h + 1, :] - log_col[:, h : h + 1]
        decay = jnp.exp(jnp.where(upper, gaps, -1e30))
        mine = slice(h * width, (h + 1) * width)
        weighted = decay * dot(stepped[:, mine], out_back_bf[:, mine], NT)
        group_pair = group_pair + weighted
        terms = weighted * mix_dot
        later.append(jnp.sum(terms, axis=0, keepdims=True))
        earlier.append(jnp.sum(terms, axis=1, keepdims=True))
        parts.append(dot((decay * mix_dot).astype(bf16), out_back_bf[:, mine]))
    adj_ref[...] = jnp.concatenate(parts, axis=1)
    begin = begin_ref[...]
    decayed = out_back * spread(jnp.exp(log_cum), owner)
    pair_bf = group_pair.astype(bf16)
    in_ref[...] = dot(mix_out, pair_bf, NT)
    out_ref[...] = dot(mix_in, pair_bf) + dot(begin.astype(bf16), decayed.astype(bf16), NT)
    from_state = dot(mix_out.astype(f32), begin, TN)
    net = jnp.concatenate(later, axis=0) - jnp.concatenate(earlier, axis=1).T
    net = net + head_sums(owner, decayed * from_state)
    log_ref[...] = dot(net, (row >= col).astype(f32), precision=highest)


def scan_pairs(x, out_back, mix_in, mix_out, step, rate, begin):
    length, channels = x.shape
    heads = step.shape[0]
    states = mix_out.shape[1]
    blocks = length // BLOCK
    whole = lambda shape: pl.BlockSpec(shape, lambda b: (0,) * len(shape))
    rows = pl.BlockSpec((BLOCK, channels), lambda b: (b, 0))
    mix = pl.BlockSpec(squeezed(states, BLOCK), lambda b: (0, 0, b))
    line = pl.BlockSpec((heads, BLOCK), lambda b: (0, b))
    return pl.pallas_call(
        pairs_body,
        grid=(blocks,),
        in_specs=[rows, rows, mix, mix, line, whole((1, heads)),
                  pl.BlockSpec(squeezed(states, channels), lambda b: (b, 0, 0))],
        out_specs=[rows, mix, mix, line],
        out_shape=[jax.ShapeDtypeStruct((length, channels), f32),
                   jax.ShapeDtypeStruct((1, states, length), f32),
                   jax.ShapeDtypeStruct((1, states, length), f32),
                   jax.ShapeDtypeStruct((heads, length), f32)],
        compiler_params=limits(28),
        cost_estimate=cost(11),
        name="scan_pairs",
    )(x, out_back, mix_in, mix_out, step, rate, begin)


def finish_body(place_ref, x_ref, ob_ref, adj_ref, b_ref, step_ref, rate_ref, skip_ref, begin_ref, end_ref,
                in_part_ref, log_part_ref, joined_ref,
                grad_ref, in_ref, step_grad_ref, carried_ref):
    heads, tokens = step_ref.shape
    channels = x_ref.shape[1]

    @pl.when(pl.program_id(0) == 0)
    def _():
        states = carried_ref.shape[0]
        incoming = jnp.zeros(carried_ref.shape, f32)
        for k in range(joined_ref.shape[0] - 1, 0, -1):
            joined = joined_ref[k].astype(f32)
            further = joined[:states] + joined[states:] * incoming
            incoming = jnp.where(place_ref[2] < k, further, incoming)
        carried_ref[...] = incoming

    owner = head_of_channel(heads, channels)
    x = x_ref[...].astype(f32)
    step = step_ref[...]
    rate = as_column(rate_ref[...])
    log_cum = log_cumulative(step, rate)
    last = log_cum[:, tokens - 1 :]
    carried = carried_ref[...]
    end = end_ref[...] + carried
    mix_in = b_ref[...]
    end_decay = spread(jnp.exp(last - log_cum), owner)
    stepped = spread(step, owner)
    end_back = dot(mix_in.astype(f32), end, TN) * end_decay
    adjoint = adj_ref[...] + end_back
    grad_ref[...] = (head_row(owner, as_column(skip_ref[...])) * ob_ref[...] + stepped * adjoint).astype(bf16)
    in_ref[...] = in_part_ref[...] + dot(end.astype(bf16), (stepped * end_decay * x).astype(bf16), NT)
    end_term = step * head_sums(owner, x * end_back)
    row = lax.broadcasted_iota(jnp.int32, (tokens, tokens), 0)
    col = lax.broadcasted_iota(jnp.int32, (tokens, tokens), 1)
    block_decay = jnp.exp(last)
    both = jnp.sum(end * begin_ref[...], axis=0, keepdims=True)
    whole_term = block_decay * jnp.sum(owner.astype(f32) * both, axis=1, keepdims=True)
    log_grad = log_part_ref[...] + dot(end_term, (row < col).astype(f32), precision=highest) + whole_term
    step_grad_ref[...] = head_sums(owner, x * adjoint) - rate * log_grad
    carried_ref[...] = head_row(owner, block_decay) * carried


def scan_finish(place, x, out_back, adjoint, mix_in, step, rate, skip, begin, end, in_part, log_part, joined):
    length, channels = x.shape
    heads = step.shape[0]
    states = mix_in.shape[1]
    blocks = length // BLOCK
    last = blocks - 1
    whole = lambda shape: pl.BlockSpec(shape, lambda b, place: (0,) * len(shape))
    rows = pl.BlockSpec((BLOCK, channels), lambda b, place: (last - b, 0))
    mix = pl.BlockSpec(squeezed(states, BLOCK), lambda b, place: (0, 0, last - b))
    line = pl.BlockSpec((heads, BLOCK), lambda b, place: (0, last - b))
    state = pl.BlockSpec(squeezed(states, channels), lambda b, place: (last - b, 0, 0))
    return pl.pallas_call(
        finish_body,
        grid_spec=pltpu.PrefetchScalarGridSpec(
            num_scalar_prefetch=1,
            grid=(blocks,),
            in_specs=[rows, rows, rows, mix, line, whole((1, heads)), whole((1, heads)), state, state,
                  mix, line, whole(joined.shape)],
            out_specs=[rows, mix, line],
            scratch_shapes=[pltpu.VMEM((states, channels), f32)],
        ),
        out_shape=[jax.ShapeDtypeStruct((length, channels), bf16),
                   jax.ShapeDtypeStruct((1, states, length), f32),
                   jax.ShapeDtypeStruct((heads, length), f32)],
        compiler_params=limits(24),
        cost_estimate=cost(9),
        name="scan_finish",
    )(place, x, out_back, adjoint, mix_in, step, rate, skip, begin, end, in_part, log_part, joined)


CHUNKS = 8
OFFSETS = (0, -1, 1, 2)


def shifted(value, axis, by):
    size = lax.axis_size(axis)
    return lax.ppermute(value, axis, [(k, (k + by) % size) for k in range(size)])


def swapped(value):
    return shifted(value, "exp_1", 1)


def ring_pieces(rows):
    half = rows.shape[0] // 2
    right = shifted(rows, "exp_0", 1)
    left = shifted(rows, "exp_0", -1)
    ahead = shifted(right[:half], "exp_0", 1)
    behind = shifted(left[half:], "exp_0", -1)
    local = [rows, right, left, ahead, behind]
    return local + [swapped(piece) for piece in local]


def chunk_index(place_ref, slot):
    chip, core = place_ref[0], place_ref[1]
    return (chip + OFFSETS[slot % 4] + 4) % 4 * 2 + (core + slot // 4) % 2


def chunk_values(refs, slot):
    side, turn = slot // 4 * 5, slot % 4
    if turn < 3:
        return refs[side + turn][...]
    return jnp.concatenate([refs[side + 3][...], refs[side + 4][...]], axis=0)


def fill_ranks(share_ref, rank_ref):
    @pl.when(pl.program_id(0) == 0)
    def _():
        rank_all(share_ref, rank_ref)


def rank_all(share_ref, rank_ref):
    hit = (share_ref[...] > 0).astype(f32)
    tokens = hit.shape[1]
    row = lax.broadcasted_iota(jnp.int32, (tokens, tokens), 0)
    col = lax.broadcasted_iota(jnp.int32, (tokens, tokens), 1)
    before = dot(hit.astype(bf16), (row < col).astype(bf16))
    rank_ref[...] = jnp.where(hit > 0, before, -1.0)


def slots_of(rank_ref, index, capacity):
    rank = rank_ref[pl.ds(index, 1), :]
    place = lax.broadcasted_iota(jnp.int32, (capacity, rank.shape[1]), 0).astype(f32)
    return place == rank


def collect_body(scaled, place_ref, share_ref, *refs):
    pieces, out_ref, rank_ref = refs[:10], refs[10], refs[11]
    capacity = out_ref.shape[0] // CHUNKS
    fill_ranks(share_ref, rank_ref)
    for slot in range(CHUNKS):
        index = chunk_index(place_ref, slot)
        chosen = slots_of(rank_ref, index, capacity)
        rows = dot(chosen.astype(bf16), chunk_values(pieces, slot))
        if scaled:
            share = share_ref[pl.ds(index, 1), :]
            rows = rows * jnp.sum(jnp.where(chosen, share, 0.0), axis=1, keepdims=True)
        out_ref[slot * capacity : (slot + 1) * capacity, :] = rows.astype(bf16)


def column_call(body, inputs, out_shape, scratch, name, mib, micros):
    place, share, *arrays = inputs
    width = arrays[0].shape[1]
    tiles = 4
    cut = lambda leaf: pl.BlockSpec((leaf.shape[0], width // tiles), lambda i, place: (0, i))
    return pl.pallas_call(
        body,
        grid_spec=pltpu.PrefetchScalarGridSpec(
            num_scalar_prefetch=1,
            grid=(tiles,),
            in_specs=[pl.BlockSpec(share.shape, lambda i, place: (0, 0))] + [cut(leaf) for leaf in arrays],
            out_specs=jax.tree.map(cut, out_shape),
            scratch_shapes=scratch,
        ),
        out_shape=out_shape,
        compiler_params=limits(mib),
        cost_estimate=cost(micros),
        name=name,
    )(place, share, *arrays)


def collect(place, share, pieces, capacity, scaled):
    tokens, width = pieces[0].shape

    def body(*refs):
        collect_body(scaled, *refs)

    return column_call(
        body,
        (place, share, *pieces),
        jax.ShapeDtypeStruct((CHUNKS * capacity, width), bf16),
        [pltpu.VMEM(share.shape, f32)],
        "collect_scaled" if scaled else "collect",
        16,
        3,
    )


def deliver_body(place_ref, share_ref, rows_ref, *refs):
    outs, rank_ref = refs[:8], refs[8]
    capacity = rows_ref.shape[0] // CHUNKS
    fill_ranks(share_ref, rank_ref)
    for slot in range(CHUNKS):
        chosen = slots_of(rank_ref, chunk_index(place_ref, slot), capacity)
        rows = rows_ref[slot * capacity : (slot + 1) * capacity, :]
        outs[slot][...] = dot(chosen.astype(bf16), rows, TN).astype(bf16)


def deliver(place, share, rows):
    tokens, width = share.shape[1], rows.shape[1]
    return column_call(
        deliver_body,
        (place, share, rows),
        [jax.ShapeDtypeStruct((tokens, width), bf16)] * CHUNKS,
        [pltpu.VMEM(share.shape, f32)],
        "deliver",
        16,
        4,
    )


def returned_sum(parts, done):
    here = [part + swapped(other) for part, other in zip(parts[:4], parts[4:])]
    mine, behind, ahead, across = here
    half = mine.shape[0] // 2
    first = shifted(across[:half], "exp_0", 1)
    second = shifted(across[half:], "exp_0", -1)
    left_late = shifted(ahead[half:], "exp_0", 1)
    right_late = shifted(behind[:half], "exp_0", -1)
    first, second, _ = lax.optimization_barrier((first, second, done))
    left = shifted(ahead[:half] + first, "exp_0", 1)
    right = shifted(behind[half:] + second, "exp_0", -1)
    wide = lambda part: part.astype(f32)
    return wide(mine) + jnp.concatenate(
        [wide(left) + wide(right_late), wide(left_late) + wide(right)], axis=0
    )


def column_partials_body(left_ref, right_ref, out_ref, turned_ref):
    @pl.when(pl.program_id(0) == 0)
    def _():
        turned_ref[...] = left_ref[...].T

    product = dot(turned_ref[...], right_ref[...]).astype(bf16)
    for k in range(out_ref.shape[0]):
        out_ref[k] = product[:, k * out_ref.shape[2] : (k + 1) * out_ref.shape[2]]


def column_partials(left, right, pieces, name):
    rows, height = left.shape
    width = right.shape[1] // pieces
    return pl.pallas_call(
        column_partials_body,
        grid=(pieces // 2,),
        in_specs=[pl.BlockSpec((rows, height), lambda i: (0, 0)),
                  pl.BlockSpec((rows, 2 * width), lambda i: (0, i))],
        out_specs=pl.BlockSpec((2, height, width), lambda i: (i, 0, 0)),
        out_shape=jax.ShapeDtypeStruct((pieces, height, width), bf16),
        scratch_shapes=[pltpu.VMEM((height, rows), bf16)],
        compiler_params=limits(24),
        cost_estimate=cost(6),
        name=name,
    )(left, right)


def row_partials_body(in_ref, grad_ref, gate_ref, up_ref, hidden_ref, out_ref):
    width = gate_ref.shape[1]
    turned = in_ref[...].T
    out_ref[:, :width] = dot(turned, gate_ref[...]).astype(bf16)
    out_ref[:, width : 2 * width] = dot(turned, up_ref[...]).astype(bf16)
    out_ref[:, 2 * width :] = dot(grad_ref[...].T, hidden_ref[...]).astype(bf16)


def row_partials(rows_in, rows_grad, gate, up, hidden):
    rows, height = rows_in.shape
    width = gate.shape[1]
    tile = 512
    cut = pl.BlockSpec((rows, tile), lambda i: (0, i))
    whole = pl.BlockSpec((rows, width), lambda i: (0, 0))
    return pl.pallas_call(
        row_partials_body,
        grid=(height // tile,),
        in_specs=[cut, cut, whole, whole, whole],
        out_specs=pl.BlockSpec((tile, 3 * width), lambda i: (i, 0)),
        out_shape=jax.ShapeDtypeStruct((height, 3 * width), bf16),
        compiler_params=limits(32),
        cost_estimate=cost(9),
        name="row_partials",
    )(rows_in, rows_grad, gate, up, hidden)


def shards(
    scan_input,
    gate_input,
    input_mix,
    output_mix,
    step_size,
    decay_rate,
    skip_scale,
    norm_gain,
    entry_state,
    out_weight,
    block_mid,
    expert_gain,
    expert_choice,
    route_weight,
    gate_proj,
    up_proj,
    down_proj,
    out_grad,
):
    channels = scan_input.shape[1]
    heads = step_size.shape[0]
    states = input_mix.shape[1]
    experts = lax.axis_size(EXP)
    ranges = lax.axis_size("seq")
    tokens = block_mid.shape[0]
    capacity = 4 * tokens // experts
    place = jnp.stack([lax.axis_index(axis) for axis in ("exp_0", "exp_1", "seq")]).astype(jnp.int32)
    rate, skip, gain = decay_rate[None], skip_scale[None], norm_gain[None]

    mid_values = block_mid.astype(f32)
    mid_scale = lax.rsqrt(jnp.mean(mid_values * mid_values, axis=1, keepdims=True) + norm_eps)
    normed_mid = (mid_values * mid_scale * expert_gain).astype(bf16)
    named = expert_choice.T[None] == jnp.arange(experts, dtype=jnp.int32)[:, None, None]
    share = jnp.sum(jnp.where(named, route_weight.T[None], 0.0), axis=1)
    share = lax.all_to_all(share, EXP, 0, 0, tiled=True)
    grad_pieces = ring_pieces(out_grad)
    in_pieces = ring_pieces(normed_mid)

    y, normed, begin = scan_forward(
        scan_input, gate_input, input_mix, output_mix, step_size, rate, skip, gain,
        entry_state.reshape(channels, states),
    )
    grad_pieces, y = lax.optimization_barrier((grad_pieces, y))

    gate_matrix, up_matrix, down_matrix = gate_proj[0], up_proj[0], down_proj[0]
    rows_grad = collect(place, share, grad_pieces, capacity, True)
    hidden_back = dot(rows_grad, down_matrix, NT)
    in_pieces, hidden_back = lax.optimization_barrier((in_pieces, hidden_back))
    rows_in = collect(place, share, in_pieces, capacity, False)
    gate_pre = dot(rows_in, gate_matrix)
    up_pre = dot(rows_in, up_matrix)
    gate_act, gate_slope = silu_parts(gate_pre)
    hidden = (gate_act * up_pre).astype(bf16)
    gate_back = (hidden_back * up_pre * gate_slope).astype(bf16)
    up_back = (hidden_back * gate_act).astype(bf16)
    rows_back = dot(gate_back, gate_matrix, NT) + dot(up_back, up_matrix, NT)
    parts = deliver(place, share, rows_back.astype(bf16))
    partials = row_partials(rows_in, rows_grad, gate_back, up_back, hidden)
    summed = lax.psum_scatter(partials, "seq", scatter_dimension=0, tiled=True)

    weighted_back = returned_sum(parts, partials) * expert_gain
    mid_grad = (
        out_grad.astype(f32)
        + mid_scale * weighted_back
        - mid_values * mid_scale**3 * jnp.mean(mid_values * weighted_back, axis=1, keepdims=True)
    ).astype(bf16)
    out_back, gate_grad, end, joined, shard_rows = scan_backward(
        place, ring_pieces(mid_grad), out_weight, y, gate_input, output_mix, step_size, rate, gain
    )
    joined = lax.all_to_all(
        jnp.broadcast_to(joined[None], (ranges, *joined.shape)), "seq", 0, 0, tiled=True
    )
    out_part = column_partials(normed, shard_rows, ranges, "out_partials")
    out_parts = lax.all_to_all(out_part, "seq", 0, 0, tiled=True)
    inner, in_part, out_mix_grad, log_part = scan_pairs(
        scan_input, out_back, input_mix, output_mix, step_size, rate, begin
    )
    joined, inner = lax.optimization_barrier((joined, inner))
    input_grad, in_mix_grad, step_grad = scan_finish(
        place, scan_input, out_back, inner, input_mix, step_size, rate, skip, begin, end,
        in_part, log_part, joined,
    )
    width = gate_back.shape[1]
    summed = summed.astype(f32)
    return (
        mid_grad,
        input_grad,
        gate_grad,
        in_mix_grad,
        out_mix_grad,
        step_grad,
        jnp.sum(out_parts.astype(f32), axis=0),
        summed[None, :, :width],
        summed[None, :, width : 2 * width],
        summed[None, :, 2 * width :].transpose(0, 2, 1),
    )


def solution(mesh):
    split = Mesh(mesh.devices.reshape(mesh.shape["seq"], 4, 2), ("seq", "exp_0", "exp_1"))
    placed = (
        P("seq", EXP),
        P("seq", EXP),
        P(EXP, None, "seq"),
        P(EXP, None, "seq"),
        P(EXP, "seq"),
        P(EXP),
        P(EXP),
        P(EXP),
        P("seq", EXP, None, None),
        P(EXP, None),
        P(SEQ_EXP, None),
        P(),
        P(SEQ_EXP, None),
        P(SEQ_EXP, None),
        P(EXP, None, None),
        P(EXP, None, None),
        P(EXP, None, None),
        P(SEQ_EXP, None),
    )
    return jax.shard_map(
        shards,
        mesh=split,
        in_specs=placed,
        out_specs=(
            P(SEQ_EXP, None),
            P("seq", EXP),
            P("seq", EXP),
            P(EXP, None, "seq"),
            P(EXP, None, "seq"),
            P(EXP, "seq"),
            P(EXP, "seq"),
            P(EXP, "seq", None),
            P(EXP, "seq", None),
            P(EXP, None, "seq"),
        ),
        check_vma=False,
    )
```

```python
import jax
import jax.numpy as jnp
from jax import lax
from jax.experimental import pallas as pl
from jax.experimental.pallas import tpu as pltpu
from jax.sharding import Mesh
from jax.sharding import PartitionSpec as P

BLOCK = 256
EXP = ("exp_0", "exp_1")
SEQ_EXP = ("seq", "exp_0", "exp_1")
norm_eps = 1e-05
highest = lax.Precision.HIGHEST
f32 = jnp.float32
bf16 = jnp.bfloat16


def dot(a, b, dims=((1,), (0,)), precision=None):
    return lax.dot_general(a, b, (dims, ((), ())), preferred_element_type=f32, precision=precision)


NT = ((1,), (1,))
TN = ((0,), (0,))


def split_two(value):
    high = value.astype(bf16)
    return high, (value - high.astype(f32)).astype(bf16)


def head_of_channel(heads, channels):
    row = lax.broadcasted_iota(jnp.int32, (heads, channels), 0)
    col = lax.broadcasted_iota(jnp.int32, (heads, channels), 1)
    return (col // (channels // heads) == row).astype(bf16)


def spread(per_head, owner):
    high, low = split_two(per_head)
    return dot(high, owner, TN) + dot(low, owner, TN)


def head_sums(owner, value):
    high, low = split_two(value)
    return dot(owner, high, NT) + dot(owner, low, NT)


def as_column(row):
    size = row.shape[1]
    same = lax.broadcasted_iota(jnp.int32, (size, size), 0) == lax.broadcasted_iota(jnp.int32, (size, size), 1)
    return jnp.sum(jnp.where(same, row, 0.0), axis=1, keepdims=True)


def limits(mib):
    return pltpu.CompilerParams(vmem_limit_bytes=mib << 20)


def cost(micros):
    return pl.CostEstimate(flops=int(micros * 9e8), transcendentals=0, bytes_accessed=int(micros * 2e6))


def head_row(owner, column):
    return jnp.sum(owner.astype(f32) * column, axis=0, keepdims=True)


def triangle_sums(rows, triangle):
    count = rows.shape[0]
    high, rest = rows.astype(bf16), rows - rows.astype(bf16).astype(f32)
    middle, low = split_two(rest)
    three = dot(jnp.concatenate([high.astype(f32), middle.astype(f32), low.astype(f32)], axis=0).astype(bf16),
                triangle.astype(bf16))
    return three[:count] + three[count : 2 * count] + three[2 * count :]


def log_cumulative(step, rate):
    tokens = step.shape[1]
    row = lax.broadcasted_iota(jnp.int32, (tokens, tokens), 0)
    col = lax.broadcasted_iota(jnp.int32, (tokens, tokens), 1)
    return triangle_sums(-step * rate, (row <= col).astype(f32))


def silu_parts(values):
    sigmoid = 1.0 / (1.0 + jnp.exp(-values))
    return values * sigmoid, sigmoid * (1.0 + values * (1.0 - sigmoid))


def forward_body(x_ref, z_ref, b_ref, c_ref, step_ref, rate_ref, skip_ref, gain_ref, entry_ref,
                 y_ref, normed_ref, begin_ref, state_ref):
    heads, tokens = step_ref.shape
    channels = x_ref.shape[1]
    width = channels // heads

    @pl.when(pl.program_id(0) == 0)
    def _():
        state_ref[...] = entry_ref[...].T

    owner = head_of_channel(heads, channels)
    x = x_ref[...].astype(f32)
    step = step_ref[...]
    log_cum = log_cumulative(step, as_column(rate_ref[...]))
    log_col = log_cum.T
    mix_in, mix_out = b_ref[...], c_ref[...]
    stepped = x * spread(step, owner)
    stepped_bf = stepped.astype(bf16)
    mix_dot = dot(mix_out, mix_in, TN)
    row = lax.broadcasted_iota(jnp.int32, (tokens, tokens), 0)
    col = lax.broadcasted_iota(jnp.int32, (tokens, tokens), 1)
    lower = row >= col
    parts = []
    for h in range(heads):
        gaps = log_col[:, h : h + 1] - log_cum[h : h + 1, :]
        kernel = (jnp.exp(jnp.where(lower, gaps, -1e30)) * mix_dot).astype(bf16)
        parts.append(dot(kernel, stepped_bf[:, h * width : (h + 1) * width]))
    state = state_ref[...]
    begin_ref[...] = state
    from_state = dot(mix_out.astype(f32), state, TN) * spread(jnp.exp(log_cum), owner)
    y = jnp.concatenate(parts, axis=1) + from_state + head_row(owner, as_column(skip_ref[...])) * x
    y_ref[...] = y
    last = log_cum[:, tokens - 1 :]
    ended = (stepped * spread(jnp.exp(last - log_cum), owner)).astype(bf16)
    state_ref[...] = head_row(owner, jnp.exp(last)) * state + dot(mix_in, ended)
    gate_act, _ = silu_parts(z_ref[...].astype(f32))
    gated = y * gate_act
    scale = lax.rsqrt(jnp.mean(gated * gated, axis=1, keepdims=True) + norm_eps)
    normed_ref[...] = (gated * scale * gain_ref[...]).astype(bf16)


def squeezed(*shape):
    return (pl.Squeezed(), *shape)


def scan_forward(x, z, mix_in, mix_out, step, rate, skip, gain, entry):
    length, channels = x.shape
    heads = step.shape[0]
    states = mix_in.shape[1]
    blocks = length // BLOCK
    whole = lambda shape: pl.BlockSpec(shape, lambda b: (0,) * len(shape))
    rows = pl.BlockSpec((BLOCK, channels), lambda b: (b, 0))
    mix = pl.BlockSpec(squeezed(states, BLOCK), lambda b: (0, 0, b))
    return pl.pallas_call(
        forward_body,
        grid=(blocks,),
        in_specs=[rows, rows, mix, mix, pl.BlockSpec((heads, BLOCK), lambda b: (0, b)),
                  whole((1, heads)), whole((1, heads)), whole((1, channels)), whole((channels, states))],
        out_specs=[rows, rows, pl.BlockSpec(squeezed(states, channels), lambda b: (b, 0, 0))],
        out_shape=[jax.ShapeDtypeStruct((length, channels), f32),
                   jax.ShapeDtypeStruct((length, channels), bf16),
                   jax.ShapeDtypeStruct((blocks, states, channels), f32)],
        scratch_shapes=[pltpu.VMEM((states, channels), f32)],
        compiler_params=limits(56),
        cost_estimate=cost(9),
        name="scan_forward",
    )(x, z, mix_in, mix_out, step, rate, skip, gain, entry)


def backward_body(place_ref, *refs):
    pieces = refs[:10]
    (weight_ref, y_ref, z_ref, c_ref, step_ref, rate_ref, gain_ref,
     out_back_ref, gate_grad_ref, end_ref, joined_ref, rows_ref, state_ref, decay_ref, all_ref) = refs[10:]
    heads, tokens = step_ref.shape
    channels = y_ref.shape[1]
    states = state_ref.shape[0]

    @pl.when(pl.program_id(0) == 0)
    def _():
        state_ref[...] = jnp.zeros_like(state_ref)
        decay_ref[...] = jnp.ones_like(decay_ref)
        count = pieces[0].shape[0]
        half = count // 2
        for side in range(2):
            for turn in range(5):
                start = chunk_index(place_ref, side * 4 + min(turn, 3)) * count + (half if turn == 4 else 0)
                piece = pieces[side * 5 + turn]
                all_ref[pl.ds(pl.multiple_of(start, half), piece.shape[0]), :] = piece[...]

    owner = head_of_channel(heads, channels)
    log_cum = log_cumulative(step_ref[...], as_column(rate_ref[...]))
    block = pl.num_programs(0) - 1 - pl.program_id(0)
    rows = all_ref[pl.ds(pl.multiple_of(block * tokens, tokens), tokens), :]
    rows_ref[...] = rows
    projected = dot(rows, weight_ref[...], NT)
    y = y_ref[...]
    gate_act, gate_slope = silu_parts(z_ref[...].astype(f32))
    gated = y * gate_act
    scale = lax.rsqrt(jnp.mean(gated * gated, axis=1, keepdims=True) + norm_eps)
    scaled = projected * gain_ref[...]
    inner = jnp.mean(gated * scaled, axis=1, keepdims=True)
    gated_back = scale * scaled - gated * (scale * scale * scale * inner)
    out_back = gated_back * gate_act
    gate_grad_ref[...] = (gated_back * y * gate_slope).astype(bf16)
    out_back_ref[...] = out_back
    state = state_ref[...]
    end_ref[...] = state
    decayed = (out_back * spread(jnp.exp(log_cum), owner)).astype(bf16)
    block_decay = head_row(owner, jnp.exp(log_cum[:, tokens - 1 :]))
    state = block_decay * state + dot(c_ref[...], decayed)
    decay = block_decay * decay_ref[...]
    state_ref[...] = state
    decay_ref[...] = decay
    joined_ref[:states, :] = state.astype(bf16)
    joined_ref[states:, :] = decay.astype(bf16)


def scan_backward(place, pieces, weight, y, z, mix_out, step, rate, gain):
    length, channels = y.shape
    heads = step.shape[0]
    states = mix_out.shape[1]
    blocks = length // BLOCK
    last = blocks - 1
    width = weight.shape[1]
    whole = lambda shape: pl.BlockSpec(shape, lambda b, place: (0,) * len(shape))
    rows = pl.BlockSpec((BLOCK, channels), lambda b, place: (last - b, 0))
    mix = pl.BlockSpec(squeezed(states, BLOCK), lambda b, place: (0, 0, last - b))
    return pl.pallas_call(
        backward_body,
        grid_spec=pltpu.PrefetchScalarGridSpec(
            num_scalar_prefetch=1,
            grid=(blocks,),
            in_specs=[whole(piece.shape) for piece in pieces] + [
                whole(weight.shape), rows, rows, mix,
                pl.BlockSpec((heads, BLOCK), lambda b, place: (0, last - b)),
                whole((1, heads)), whole((1, channels))],
            out_specs=[rows, rows, pl.BlockSpec(squeezed(states, channels), lambda b, place: (last - b, 0, 0)),
                       whole((states + 1, channels)),
                       pl.BlockSpec((BLOCK, width), lambda b, place: (last - b, 0))],
            scratch_shapes=[pltpu.VMEM((states, channels), f32), pltpu.VMEM((1, channels), f32),
                            pltpu.VMEM((length, width), bf16)],
        ),
        out_shape=[jax.ShapeDtypeStruct((length, channels), f32),
                   jax.ShapeDtypeStruct((length, channels), bf16),
                   jax.ShapeDtypeStruct((blocks, states, channels), f32),
                   jax.ShapeDtypeStruct((states + 1, channels), bf16),
                   jax.ShapeDtypeStruct((length, width), bf16)],
        compiler_params=limits(56),
        cost_estimate=cost(9),
        name="scan_backward",
    )(place, *pieces, weight, y, z, mix_out, step, rate, gain)


def pairs_body(x_ref, ob_ref, b_ref, c_ref, step_ref, rate_ref, begin_ref,
               adj_ref, in_ref, out_ref, log_ref):
    heads, tokens = step_ref.shape
    channels = x_ref.shape[1]
    width = channels // heads
    owner = head_of_channel(heads, channels)
    step = step_ref[...]
    log_cum = log_cumulative(step, as_column(rate_ref[...]))
    log_col = log_cum.T
    mix_in, mix_out = b_ref[...], c_ref[...]
    out_back = ob_ref[...]
    out_back_bf = out_back.astype(bf16)
    stepped = (x_ref[...].astype(f32) * spread(step, owner)).astype(bf16)
    mix_dot = dot(mix_in, mix_out, TN)
    row = lax.broadcasted_iota(jnp.int32, (tokens, tokens), 0)
    col = lax.broadcasted_iota(jnp.int32, (tokens, tokens), 1)
    upper = row <= col
    group_pair = jnp.zeros((tokens, tokens), f32)
    parts, later, earlier = [], [], []
    for h in range(heads):
        gaps = log_cum[h : h + 1, :] - log_col[:, h : h + 1]
        decay = jnp.exp(jnp.where(upper, gaps, -1e30))
        mine = slice(h * width, (h + 1) * width)
        weighted = decay * dot(stepped[:, mine], out_back_bf[:, mine], NT)
        group_pair = group_pair + weighted
        terms = weighted * mix_dot
        later.append(jnp.sum(terms, axis=0, keepdims=True))
        earlier.append(jnp.sum(terms, axis=1, keepdims=True))
        parts.append(dot((decay * mix_dot).astype(bf16), out_back_bf[:, mine]))
    adj_ref[...] = jnp.concatenate(parts, axis=1)
    begin = begin_ref[...]
    decayed = out_back * spread(jnp.exp(log_cum), owner)
    pair_bf = group_pair.astype(bf16)
    in_ref[...] = dot(mix_out, pair_bf, NT)
    out_ref[...] = dot(mix_in, pair_bf) + dot(begin.astype(bf16), decayed.astype(bf16), NT)
    from_state = dot(mix_out.astype(f32), begin, TN)
    net = jnp.concatenate(later, axis=0) - jnp.concatenate(earlier, axis=1).T
    net = net + head_sums(owner, decayed * from_state)
    log_ref[...] = triangle_sums(net, (row >= col).astype(f32))


def scan_pairs(x, out_back, mix_in, mix_out, step, rate, begin):
    length, channels = x.shape
    heads = step.shape[0]
    states = mix_out.shape[1]
    blocks = length // BLOCK
    whole = lambda shape: pl.BlockSpec(shape, lambda b: (0,) * len(shape))
    rows = pl.BlockSpec((BLOCK, channels), lambda b: (b, 0))
    mix = pl.BlockSpec(squeezed(states, BLOCK), lambda b: (0, 0, b))
    line = pl.BlockSpec((heads, BLOCK), lambda b: (0, b))
    return pl.pallas_call(
        pairs_body,
        grid=(blocks,),
        in_specs=[rows, rows, mix, mix, line, whole((1, heads)),
                  pl.BlockSpec(squeezed(states, channels), lambda b: (b, 0, 0))],
        out_specs=[rows, mix, mix, line],
        out_shape=[jax.ShapeDtypeStruct((length, channels), f32),
                   jax.ShapeDtypeStruct((1, states, length), f32),
                   jax.ShapeDtypeStruct((1, states, length), f32),
                   jax.ShapeDtypeStruct((heads, length), f32)],
        compiler_params=limits(56),
        cost_estimate=cost(11),
        name="scan_pairs",
    )(x, out_back, mix_in, mix_out, step, rate, begin)


def finish_body(place_ref, x_ref, ob_ref, adj_ref, b_ref, step_ref, rate_ref, skip_ref, begin_ref, end_ref,
                in_part_ref, log_part_ref, joined_ref,
                grad_ref, in_ref, step_grad_ref, carried_ref):
    heads, tokens = step_ref.shape
    channels = x_ref.shape[1]

    @pl.when(pl.program_id(0) == 0)
    def _():
        states = carried_ref.shape[0]
        incoming = jnp.zeros(carried_ref.shape, f32)
        lines = channels // joined_ref.shape[2]
        for k in range(joined_ref.shape[0] - 1, 0, -1):
            joined = joined_ref[k].astype(f32)
            adjoint = jnp.concatenate([joined[q * states : (q + 1) * states] for q in range(lines)], axis=1)
            decay = jnp.concatenate(
                [joined[lines * states + q : lines * states + q + 1] for q in range(lines)], axis=1)
            further = adjoint + decay * incoming
            incoming = jnp.where(place_ref[2] < k, further, incoming)
        carried_ref[...] = incoming

    owner = head_of_channel(heads, channels)
    x = x_ref[...].astype(f32)
    step = step_ref[...]
    rate = as_column(rate_ref[...])
    log_cum = log_cumulative(step, rate)
    last = log_cum[:, tokens - 1 :]
    carried = carried_ref[...]
    end = end_ref[...] + carried
    mix_in = b_ref[...]
    end_decay = spread(jnp.exp(last - log_cum), owner)
    stepped = spread(step, owner)
    end_back = dot(mix_in.astype(f32), end, TN) * end_decay
    adjoint = adj_ref[...] + end_back
    grad_ref[...] = (head_row(owner, as_column(skip_ref[...])) * ob_ref[...] + stepped * adjoint).astype(bf16)
    in_ref[...] = in_part_ref[...] + dot(end.astype(bf16), (stepped * end_decay * x).astype(bf16), NT)
    end_term = step * head_sums(owner, x * end_back)
    row = lax.broadcasted_iota(jnp.int32, (tokens, tokens), 0)
    col = lax.broadcasted_iota(jnp.int32, (tokens, tokens), 1)
    block_decay = jnp.exp(last)
    both = jnp.sum(end * begin_ref[...], axis=0, keepdims=True)
    whole_term = block_decay * jnp.sum(owner.astype(f32) * both, axis=1, keepdims=True)
    log_grad = log_part_ref[...] + triangle_sums(end_term, (row < col).astype(f32)) + whole_term
    step_grad_ref[...] = head_sums(owner, x * adjoint) - rate * log_grad
    carried_ref[...] = head_row(owner, block_decay) * carried


def scan_finish(place, x, out_back, adjoint, mix_in, step, rate, skip, begin, end, in_part, log_part, joined):
    length, channels = x.shape
    heads = step.shape[0]
    states = mix_in.shape[1]
    blocks = length // BLOCK
    last = blocks - 1
    whole = lambda shape: pl.BlockSpec(shape, lambda b, place: (0,) * len(shape))
    rows = pl.BlockSpec((BLOCK, channels), lambda b, place: (last - b, 0))
    mix = pl.BlockSpec(squeezed(states, BLOCK), lambda b, place: (0, 0, last - b))
    line = pl.BlockSpec((heads, BLOCK), lambda b, place: (0, last - b))
    state = pl.BlockSpec(squeezed(states, channels), lambda b, place: (last - b, 0, 0))
    return pl.pallas_call(
        finish_body,
        grid_spec=pltpu.PrefetchScalarGridSpec(
            num_scalar_prefetch=1,
            grid=(blocks,),
            in_specs=[rows, rows, rows, mix, line, whole((1, heads)), whole((1, heads)), state, state,
                  mix, line, whole(joined.shape)],
            out_specs=[rows, mix, line],
            scratch_shapes=[pltpu.VMEM((states, channels), f32)],
        ),
        out_shape=[jax.ShapeDtypeStruct((length, channels), bf16),
                   jax.ShapeDtypeStruct((1, states, length), f32),
                   jax.ShapeDtypeStruct((heads, length), f32)],
        compiler_params=limits(56),
        cost_estimate=cost(9),
        name="scan_finish",
    )(place, x, out_back, adjoint, mix_in, step, rate, skip, begin, end, in_part, log_part, joined)


CHUNKS = 8
OFFSETS = (0, -1, 1, 2)


def shifted(value, axis, by):
    size = lax.axis_size(axis)
    return lax.ppermute(value, axis, [(k, (k + by) % size) for k in range(size)])


def swapped(value):
    return shifted(value, "exp_1", 1)


def ring_pieces(rows):
    half = rows.shape[0] // 2
    right = shifted(rows, "exp_0", 1)
    left = shifted(rows, "exp_0", -1)
    ahead = shifted(right[:half], "exp_0", 1)
    behind = shifted(left[half:], "exp_0", -1)
    local = [rows, right, left, ahead, behind]
    return local + [swapped(piece) for piece in local]


def chunk_index(place_ref, slot):
    chip, core = place_ref[0], place_ref[1]
    return (chip + OFFSETS[slot % 4] + 4) % 4 * 2 + (core + slot // 4) % 2


def chunk_values(refs, slot):
    side, turn = slot // 4 * 5, slot % 4
    if turn < 3:
        return refs[side + turn][...]
    return jnp.concatenate([refs[side + 3][...], refs[side + 4][...]], axis=0)


PARTS = 3
EXTRA = 128


def payload_body(mid_ref, gain_ref, choice_ref, weight_ref, out_ref):
    width = mid_ref.shape[1]
    mid = mid_ref[...].astype(f32)
    scale = lax.rsqrt(jnp.mean(mid * mid, axis=1, keepdims=True) + norm_eps)
    out_ref[:, :width] = (mid * scale * gain_ref[...]).astype(bf16)
    tokens = choice_ref.shape[1]
    lines = jnp.concatenate(
        [choice_ref[...].astype(f32), weight_ref[...], jnp.zeros((4, tokens), f32)], axis=0
    ).T
    lane = lax.broadcasted_iota(jnp.int32, (tokens, EXTRA), 1)
    owner, part = (lane // PARTS).astype(f32), lane % PARTS
    held = jnp.zeros((tokens, EXTRA), f32)
    for k in range(2):
        share = lines[:, 2 + k : 3 + k]
        high = share.astype(bf16).astype(f32)
        middle = (share - high).astype(bf16).astype(f32)
        low = share - high - middle
        value = jnp.where(part == 0, high, jnp.where(part == 1, middle, low))
        held = held + jnp.where(owner == lines[:, k : k + 1], value, 0.0)
    out_ref[:, width:] = held.astype(bf16)


def payload(mid, gain, choice, weight):
    tokens, width = mid.shape
    return pl.pallas_call(
        payload_body,
        out_shape=jax.ShapeDtypeStruct((tokens, width + EXTRA), bf16),
        compiler_params=limits(16),
        cost_estimate=cost(2),
        name="payload",
    )(mid, gain, choice, weight)


def slots_of(share, capacity):
    tokens = share.shape[1]
    hit = share > 0
    row = lax.broadcasted_iota(jnp.int32, (tokens, tokens), 0)
    col = lax.broadcasted_iota(jnp.int32, (tokens, tokens), 1)
    before = dot(hit.astype(f32).astype(bf16), (row < col).astype(f32).astype(bf16))
    rank = jnp.where(hit, before, -1.0)
    place = lax.broadcasted_iota(jnp.int32, (capacity, tokens), 0).astype(f32)
    return [place == rank[slot : slot + 1] for slot in range(share.shape[0])]


def collect_body(place_ref, *refs):
    pieces, extras, out_ref, share_ref = refs[:10], refs[10:20], refs[20], refs[21]
    capacity = out_ref.shape[0] // CHUNKS
    lane = lax.broadcasted_iota(jnp.int32, (8, EXTRA), 1)
    mine = (lane // PARTS == place_ref[0] * 2 + place_ref[1]).astype(f32).astype(bf16)
    share = jnp.concatenate(
        [dot(mine, chunk_values(extras, slot), NT)[:1] for slot in range(CHUNKS)], axis=0
    )
    share_ref[...] = share
    for slot, chosen in enumerate(slots_of(share, capacity)):
        rows = dot(chosen.astype(f32).astype(bf16), chunk_values(pieces, slot))
        out_ref[slot * capacity : (slot + 1) * capacity, :] = rows.astype(bf16)


TILES = 4


def collect(place, pieces, capacity):
    width = pieces[0].shape[1] - EXTRA
    tokens = pieces[0].shape[0]
    tile = width // TILES
    cut = lambda rows: pl.BlockSpec((rows, tile), lambda i, place: (0, i))
    extra = lambda rows: pl.BlockSpec((rows, EXTRA), lambda i, place: (0, width // EXTRA))
    return pl.pallas_call(
        collect_body,
        grid_spec=pltpu.PrefetchScalarGridSpec(
            num_scalar_prefetch=1,
            grid=(TILES,),
            in_specs=[cut(leaf.shape[0]) for leaf in pieces] + [extra(leaf.shape[0]) for leaf in pieces],
            out_specs=[cut(CHUNKS * capacity), pl.BlockSpec((CHUNKS, tokens), lambda i, place: (0, 0))],
        ),
        out_shape=[jax.ShapeDtypeStruct((CHUNKS * capacity, width), bf16),
                   jax.ShapeDtypeStruct((CHUNKS, tokens), f32)],
        compiler_params=limits(16),
        cost_estimate=cost(4),
        name="collect",
    )(place, *pieces, *pieces)


def collect_scaled_body(share_ref, *refs):
    pieces, out_ref = refs[:10], refs[10]
    capacity = out_ref.shape[0] // CHUNKS
    share = share_ref[...]
    for slot, chosen in enumerate(slots_of(share, capacity)):
        rows = dot(chosen.astype(f32).astype(bf16), chunk_values(pieces, slot))
        weight = jnp.sum(jnp.where(chosen, share[slot : slot + 1], 0.0), axis=1, keepdims=True)
        out_ref[slot * capacity : (slot + 1) * capacity, :] = (rows * weight).astype(bf16)


def column_call(body, share, arrays, out_shape, name, micros):
    tile = arrays[0].shape[1] // TILES
    cut = lambda leaf: pl.BlockSpec((leaf.shape[0], tile), lambda i: (0, i))
    return pl.pallas_call(
        body,
        grid=(TILES,),
        in_specs=[pl.BlockSpec(share.shape, lambda i: (0, 0))] + [cut(leaf) for leaf in arrays],
        out_specs=jax.tree.map(cut, out_shape),
        out_shape=out_shape,
        compiler_params=limits(16),
        cost_estimate=cost(micros),
        name=name,
    )(share, *arrays)


def collect_scaled(share, pieces, capacity):
    shape = jax.ShapeDtypeStruct((CHUNKS * capacity, pieces[0].shape[1]), bf16)
    return column_call(collect_scaled_body, share, pieces, shape, "collect_scaled", 4)


def deliver_body(share_ref, rows_ref, *outs):
    capacity = rows_ref.shape[0] // CHUNKS
    for slot, chosen in enumerate(slots_of(share_ref[...], capacity)):
        rows = rows_ref[slot * capacity : (slot + 1) * capacity, :]
        outs[slot][...] = dot(chosen.astype(f32).astype(bf16), rows, TN).astype(bf16)


def deliver(share, rows):
    shape = jax.ShapeDtypeStruct((share.shape[1], rows.shape[1]), bf16)
    return column_call(deliver_body, share, [rows], [shape] * CHUNKS, "deliver", 3)


def returned_sum(parts, done):
    here = [part + swapped(other) for part, other in zip(parts[:4], parts[4:])]
    mine, behind, ahead, across = here
    half = mine.shape[0] // 2
    first = shifted(jnp.concatenate([across[:half], ahead[half:]], axis=0), "exp_0", 1)
    second = shifted(jnp.concatenate([behind[:half], across[half:]], axis=0), "exp_0", -1)
    first, second, _ = lax.optimization_barrier((first, second, done))
    left = shifted(ahead[:half] + first[:half], "exp_0", 1)
    right = shifted(behind[half:] + second[half:], "exp_0", -1)
    wide = lambda part: part.astype(f32)
    return wide(mine) + jnp.concatenate(
        [wide(left) + wide(second[:half]), wide(first[half:]) + wide(right)], axis=0
    )


def out_partials_body(left_ref, right_ref, joined_ref, out_ref, turned_ref):
    height = left_ref.shape[1]
    width = out_ref.shape[2]
    states = joined_ref.shape[0] - 1

    @pl.when(pl.program_id(0) == 0)
    def _():
        turned_ref[...] = left_ref[...].T

    product = dot(turned_ref[...], right_ref[...]).astype(bf16)
    joined = joined_ref[...]
    lines = height // width
    extra = [joined[:states, q * width : (q + 1) * width] for q in range(lines)]
    decays = jnp.concatenate(
        [joined[states:, q * width : (q + 1) * width].astype(f32) for q in range(lines)]
        + [jnp.zeros((states - lines, width), f32)], axis=0)
    for k in range(out_ref.shape[0]):
        out_ref[k, :height, :] = product[:, k * width : (k + 1) * width]
        for q in range(lines):
            out_ref[k, height + q * states : height + (q + 1) * states, :] = extra[q]
        out_ref[k, height + lines * states :, :] = decays.astype(bf16)


def out_partials(left, right, joined, pieces):
    rows, height = left.shape
    width = right.shape[1] // pieces
    states = joined.shape[0] - 1
    tall = height + (height // width + 1) * states
    return pl.pallas_call(
        out_partials_body,
        grid=(pieces // 4,),
        in_specs=[pl.BlockSpec((rows, height), lambda i: (0, 0)),
                  pl.BlockSpec((rows, 4 * width), lambda i: (0, i)),
                  pl.BlockSpec(joined.shape, lambda i: (0, 0))],
        out_specs=pl.BlockSpec((4, tall, width), lambda i: (i, 0, 0)),
        out_shape=jax.ShapeDtypeStruct((pieces, tall, width), bf16),
        scratch_shapes=[pltpu.VMEM((height, rows), bf16)],
        compiler_params=limits(56),
        cost_estimate=cost(5),
        name="out_partials",
    )(left, right, joined)


def row_partials_body(in_ref, grad_ref, gate_ref, up_ref, hidden_ref, out_ref):
    width = gate_ref.shape[1]
    turned = in_ref[...].T
    out_ref[:, :width] = dot(turned, gate_ref[...]).astype(bf16)
    out_ref[:, width : 2 * width] = dot(turned, up_ref[...]).astype(bf16)
    out_ref[:, 2 * width :] = dot(grad_ref[...].T, hidden_ref[...]).astype(bf16)


def row_partials(rows_in, rows_grad, gate, up, hidden):
    rows, height = rows_in.shape
    width = gate.shape[1]
    tile = 512
    cut = pl.BlockSpec((rows, tile), lambda i: (0, i))
    whole = pl.BlockSpec((rows, width), lambda i: (0, 0))
    return pl.pallas_call(
        row_partials_body,
        grid=(height // tile,),
        in_specs=[cut, cut, whole, whole, whole],
        out_specs=pl.BlockSpec((tile, 3 * width), lambda i: (i, 0)),
        out_shape=jax.ShapeDtypeStruct((height, 3 * width), bf16),
        compiler_params=limits(56),
        cost_estimate=cost(9),
        name="row_partials",
    )(rows_in, rows_grad, gate, up, hidden)


def shards(
    scan_input,
    gate_input,
    input_mix,
    output_mix,
    step_size,
    decay_rate,
    skip_scale,
    norm_gain,
    entry_state,
    out_weight,
    block_mid,
    expert_gain,
    expert_choice,
    route_weight,
    gate_proj,
    up_proj,
    down_proj,
    out_grad,
):
    channels = scan_input.shape[1]
    heads = step_size.shape[0]
    states = input_mix.shape[1]
    experts = lax.axis_size(EXP)
    ranges = lax.axis_size("seq")
    tokens = block_mid.shape[0]
    capacity = 4 * tokens // experts
    place = jnp.stack([lax.axis_index(axis) for axis in ("exp_0", "exp_1", "seq")]).astype(jnp.int32)
    rate, skip, gain = decay_rate[None], skip_scale[None], norm_gain[None]

    mid_values = block_mid.astype(f32)
    mid_scale = lax.rsqrt(jnp.mean(mid_values * mid_values, axis=1, keepdims=True) + norm_eps)
    in_pieces = ring_pieces(payload(block_mid, expert_gain[None], expert_choice.T, route_weight.T))
    grad_pieces = ring_pieces(out_grad)

    y, normed, begin = scan_forward(
        scan_input, gate_input, input_mix, output_mix, step_size, rate, skip, gain,
        entry_state.reshape(channels, states),
    )
    in_pieces, y = lax.optimization_barrier((in_pieces, y))

    gate_matrix, up_matrix, down_matrix = gate_proj[0], up_proj[0], down_proj[0]
    rows_in, share = collect(place, in_pieces, capacity)
    gate_pre = dot(rows_in, gate_matrix)
    up_pre = dot(rows_in, up_matrix)
    grad_pieces, up_pre = lax.optimization_barrier((grad_pieces, up_pre))
    rows_grad = collect_scaled(share, grad_pieces, capacity)
    hidden_back = dot(rows_grad, down_matrix, NT)
    gate_act, gate_slope = silu_parts(gate_pre)
    hidden = (gate_act * up_pre).astype(bf16)
    gate_back = (hidden_back * up_pre * gate_slope).astype(bf16)
    up_back = (hidden_back * gate_act).astype(bf16)
    partials = row_partials(rows_in, rows_grad, gate_back, up_back, hidden)
    gate_back, up_back, partials = lax.optimization_barrier((gate_back, up_back, partials))
    rows_back = dot(gate_back, gate_matrix, NT) + dot(up_back, up_matrix, NT)
    parts = deliver(share, rows_back.astype(bf16))
    summed = lax.psum_scatter(partials, "seq", scatter_dimension=0, tiled=True)

    weighted_back = returned_sum(parts, partials) * expert_gain
    mid_grad = (
        out_grad.astype(f32)
        + mid_scale * weighted_back
        - mid_values * mid_scale**3 * jnp.mean(mid_values * weighted_back, axis=1, keepdims=True)
    ).astype(bf16)
    out_back, gate_grad, end, joined, shard_rows = scan_backward(
        place, ring_pieces(mid_grad), out_weight, y, gate_input, output_mix, step_size, rate, gain
    )
    sent = out_partials(normed, shard_rows, joined, ranges)
    exchanged = lax.all_to_all(sent, "seq", 0, 0, tiled=True)
    inner, in_part, out_mix_grad, log_part = scan_pairs(
        scan_input, out_back, input_mix, output_mix, step_size, rate, begin
    )
    exchanged, inner = lax.optimization_barrier((exchanged, inner))
    joined = exchanged[:, channels:]
    input_grad, in_mix_grad, step_grad = scan_finish(
        place, scan_input, out_back, inner, input_mix, step_size, rate, skip, begin, end,
        in_part, log_part, joined,
    )
    width = gate_back.shape[1]
    summed = summed.astype(f32)
    return (
        mid_grad,
        input_grad,
        gate_grad,
        in_mix_grad,
        out_mix_grad,
        step_grad,
        jnp.sum(exchanged[:, :channels].astype(f32), axis=0),
        summed[None, :, :width],
        summed[None, :, width : 2 * width],
        summed[None, :, 2 * width :].transpose(0, 2, 1),
    )


def solution(mesh):
    split = Mesh(mesh.devices.reshape(mesh.shape["seq"], 4, 2), ("seq", "exp_0", "exp_1"))
    placed = (
        P("seq", EXP),
        P("seq", EXP),
        P(EXP, None, "seq"),
        P(EXP, None, "seq"),
        P(EXP, "seq"),
        P(EXP),
        P(EXP),
        P(EXP),
        P("seq", EXP, None, None),
        P(EXP, None),
        P(SEQ_EXP, None),
        P(),
        P(SEQ_EXP, None),
        P(SEQ_EXP, None),
        P(EXP, None, None),
        P(EXP, None, None),
        P(EXP, None, None),
        P(SEQ_EXP, None),
    )
    return jax.shard_map(
        shards,
        mesh=split,
        in_specs=placed,
        out_specs=(
            P(SEQ_EXP, None),
            P("seq", EXP),
            P("seq", EXP),
            P(EXP, None, "seq"),
            P(EXP, None, "seq"),
            P(EXP, "seq"),
            P(EXP, "seq"),
            P(EXP, "seq", None),
            P(EXP, "seq", None),
            P(EXP, None, "seq"),
        ),
        check_vma=False,
    )
```

```python
import jax
import jax.numpy as jnp
from jax import lax
from jax.experimental import pallas as pl
from jax.experimental.pallas import tpu as pltpu
from jax.sharding import Mesh
from jax.sharding import PartitionSpec as P

BLOCK = 256
EXP = ("exp_0", "exp_1")
SEQ_EXP = ("seq", "exp_0", "exp_1")
norm_eps = 1e-05
highest = lax.Precision.HIGHEST
f32 = jnp.float32
bf16 = jnp.bfloat16


def dot(a, b, dims=((1,), (0,)), precision=None):
    return lax.dot_general(a, b, (dims, ((), ())), preferred_element_type=f32, precision=precision)


NT = ((1,), (1,))
TN = ((0,), (0,))


def split_two(value):
    high = value.astype(bf16)
    return high, (value - high.astype(f32)).astype(bf16)


def head_of_channel(heads, channels):
    row = lax.broadcasted_iota(jnp.int32, (heads, channels), 0)
    col = lax.broadcasted_iota(jnp.int32, (heads, channels), 1)
    return (col // (channels // heads) == row).astype(bf16)


def spread(per_head, owner):
    high, low = split_two(per_head)
    return dot(high, owner, TN) + dot(low, owner, TN)


def head_sums(owner, value):
    high, low = split_two(value)
    return dot(owner, high, NT) + dot(owner, low, NT)


def as_column(row):
    size = row.shape[1]
    same = lax.broadcasted_iota(jnp.int32, (size, size), 0) == lax.broadcasted_iota(jnp.int32, (size, size), 1)
    return jnp.sum(jnp.where(same, row, 0.0), axis=1, keepdims=True)


def in_hbm(shape, kind):
    return pltpu.HBM(shape, kind)


def limits(mib):
    return pltpu.CompilerParams(vmem_limit_bytes=mib << 20)


def cost(micros):
    return pl.CostEstimate(flops=int(micros * 9e8), transcendentals=0, bytes_accessed=int(micros * 2e6))


def head_row(owner, column):
    return jnp.sum(owner.astype(f32) * column, axis=0, keepdims=True)


def triangle_sums(rows, triangle):
    count = rows.shape[0]
    high, rest = rows.astype(bf16), rows - rows.astype(bf16).astype(f32)
    middle, low = split_two(rest)
    three = dot(jnp.concatenate([high.astype(f32), middle.astype(f32), low.astype(f32)], axis=0).astype(bf16),
                triangle.astype(bf16))
    return three[:count] + three[count : 2 * count] + three[2 * count :]


def log_cumulative(step, rate):
    tokens = step.shape[1]
    row = lax.broadcasted_iota(jnp.int32, (tokens, tokens), 0)
    col = lax.broadcasted_iota(jnp.int32, (tokens, tokens), 1)
    return triangle_sums(-step * rate, (row <= col).astype(f32))


def silu_parts(values):
    sigmoid = 1.0 / (1.0 + jnp.exp(-values))
    return values * sigmoid, sigmoid * (1.0 + values * (1.0 - sigmoid))


def forward_body(x_ref, z_ref, b_ref, c_ref, step_ref, rate_ref, skip_ref, gain_ref, entry_ref,
                 y_ref, normed_ref, begin_ref, state_ref):
    heads, tokens = step_ref.shape
    channels = x_ref.shape[1]
    width = channels // heads

    @pl.when(pl.program_id(0) == 0)
    def _():
        state_ref[...] = entry_ref[...].T

    owner = head_of_channel(heads, channels)
    x = x_ref[...].astype(f32)
    step = step_ref[...]
    log_cum = log_cumulative(step, as_column(rate_ref[...]))
    log_col = log_cum.T
    mix_in, mix_out = b_ref[...], c_ref[...]
    stepped = x * spread(step, owner)
    stepped_bf = stepped.astype(bf16)
    mix_dot = dot(mix_out, mix_in, TN)
    row = lax.broadcasted_iota(jnp.int32, (tokens, tokens), 0)
    col = lax.broadcasted_iota(jnp.int32, (tokens, tokens), 1)
    lower = row >= col
    parts = []
    for h in range(heads):
        gaps = log_col[:, h : h + 1] - log_cum[h : h + 1, :]
        kernel = (jnp.exp(jnp.where(lower, gaps, -1e30)) * mix_dot).astype(bf16)
        parts.append(dot(kernel, stepped_bf[:, h * width : (h + 1) * width]))
    state = state_ref[...]
    begin_ref[...] = state
    from_state = dot(mix_out.astype(f32), state, TN) * spread(jnp.exp(log_cum), owner)
    y = jnp.concatenate(parts, axis=1) + from_state + head_row(owner, as_column(skip_ref[...])) * x
    y_ref[...] = y
    last = log_cum[:, tokens - 1 :]
    ended = (stepped * spread(jnp.exp(last - log_cum), owner)).astype(bf16)
    state_ref[...] = head_row(owner, jnp.exp(last)) * state + dot(mix_in, ended)
    gate_act, _ = silu_parts(z_ref[...].astype(f32))
    gated = y * gate_act
    scale = lax.rsqrt(jnp.mean(gated * gated, axis=1, keepdims=True) + norm_eps)
    normed_ref[...] = (gated * scale * gain_ref[...]).astype(bf16)


def squeezed(*shape):
    return (pl.Squeezed(), *shape)


def scan_forward(x, z, mix_in, mix_out, step, rate, skip, gain, entry):
    length, channels = x.shape
    heads = step.shape[0]
    states = mix_in.shape[1]
    blocks = length // BLOCK
    whole = lambda shape: pl.BlockSpec(shape, lambda b: (0,) * len(shape))
    rows = pl.BlockSpec((BLOCK, channels), lambda b: (b, 0))
    mix = pl.BlockSpec(squeezed(states, BLOCK), lambda b: (0, 0, b))
    return pl.pallas_call(
        forward_body,
        grid=(blocks,),
        in_specs=[rows, rows, mix, mix, pl.BlockSpec((heads, BLOCK), lambda b: (0, b)),
                  whole((1, heads)), whole((1, heads)), whole((1, channels)), whole((channels, states))],
        out_specs=[rows, rows, pl.BlockSpec(squeezed(states, channels), lambda b: (b, 0, 0))],
        out_shape=[in_hbm((length, channels), f32),
                   in_hbm((length, channels), bf16),
                   in_hbm((blocks, states, channels), f32)],
        scratch_shapes=[pltpu.VMEM((states, channels), f32)],
        compiler_params=limits(24),
        cost_estimate=cost(9),
        name="scan_forward",
    )(x, z, mix_in, mix_out, step, rate, skip, gain, entry)


def backward_body(place_ref, *refs):
    pieces = refs[:10]
    (weight_ref, y_ref, z_ref, c_ref, step_ref, rate_ref, gain_ref,
     out_back_ref, gate_grad_ref, end_ref, joined_ref, rows_ref, state_ref, decay_ref, all_ref) = refs[10:]
    heads, tokens = step_ref.shape
    channels = y_ref.shape[1]
    states = state_ref.shape[0]

    @pl.when(pl.program_id(0) == 0)
    def _():
        state_ref[...] = jnp.zeros_like(state_ref)
        decay_ref[...] = jnp.ones_like(decay_ref)
        count = pieces[0].shape[0]
        half = count // 2
        for side in range(2):
            for turn in range(5):
                start = chunk_index(place_ref, side * 4 + min(turn, 3)) * count + (half if turn == 4 else 0)
                piece = pieces[side * 5 + turn]
                all_ref[pl.ds(pl.multiple_of(start, half), piece.shape[0]), :] = piece[...]

    owner = head_of_channel(heads, channels)
    log_cum = log_cumulative(step_ref[...], as_column(rate_ref[...]))
    block = pl.num_programs(0) - 1 - pl.program_id(0)
    rows = all_ref[pl.ds(pl.multiple_of(block * tokens, tokens), tokens), :]
    rows_ref[...] = rows
    projected = dot(rows, weight_ref[...], NT)
    y = y_ref[...]
    gate_act, gate_slope = silu_parts(z_ref[...].astype(f32))
    gated = y * gate_act
    scale = lax.rsqrt(jnp.mean(gated * gated, axis=1, keepdims=True) + norm_eps)
    scaled = projected * gain_ref[...]
    inner = jnp.mean(gated * scaled, axis=1, keepdims=True)
    gated_back = scale * scaled - gated * (scale * scale * scale * inner)
    out_back = gated_back * gate_act
    gate_grad_ref[...] = (gated_back * y * gate_slope).astype(bf16)
    out_back_ref[...] = out_back
    state = state_ref[...]
    end_ref[...] = state
    decayed = (out_back * spread(jnp.exp(log_cum), owner)).astype(bf16)
    block_decay = head_row(owner, jnp.exp(log_cum[:, tokens - 1 :]))
    state = block_decay * state + dot(c_ref[...], decayed)
    decay = block_decay * decay_ref[...]
    state_ref[...] = state
    decay_ref[...] = decay
    joined_ref[:states, :] = state.astype(bf16)
    joined_ref[states:, :] = decay.astype(bf16)


def scan_backward(place, pieces, weight, y, z, mix_out, step, rate, gain):
    length, channels = y.shape
    heads = step.shape[0]
    states = mix_out.shape[1]
    blocks = length // BLOCK
    last = blocks - 1
    width = weight.shape[1]
    whole = lambda shape: pl.BlockSpec(shape, lambda b, place: (0,) * len(shape))
    rows = pl.BlockSpec((BLOCK, channels), lambda b, place: (last - b, 0))
    mix = pl.BlockSpec(squeezed(states, BLOCK), lambda b, place: (0, 0, last - b))
    return pl.pallas_call(
        backward_body,
        grid_spec=pltpu.PrefetchScalarGridSpec(
            num_scalar_prefetch=1,
            grid=(blocks,),
            in_specs=[whole(piece.shape) for piece in pieces] + [
                whole(weight.shape), rows, rows, mix,
                pl.BlockSpec((heads, BLOCK), lambda b, place: (0, last - b)),
                whole((1, heads)), whole((1, channels))],
            out_specs=[rows, rows, pl.BlockSpec(squeezed(states, channels), lambda b, place: (last - b, 0, 0)),
                       whole((states + 1, channels)),
                       pl.BlockSpec((BLOCK, width), lambda b, place: (last - b, 0))],
            scratch_shapes=[pltpu.VMEM((states, channels), f32), pltpu.VMEM((1, channels), f32),
                            pltpu.VMEM((length, width), bf16)],
        ),
        out_shape=[in_hbm((length, channels), f32),
                   in_hbm((length, channels), bf16),
                   in_hbm((blocks, states, channels), f32),
                   in_hbm((states + 1, channels), bf16),
                   in_hbm((length, width), bf16)],
        compiler_params=limits(36),
        cost_estimate=cost(9),
        name="scan_backward",
    )(place, *pieces, weight, y, z, mix_out, step, rate, gain)


def pairs_body(x_ref, ob_ref, b_ref, c_ref, step_ref, rate_ref, begin_ref,
               adj_ref, in_ref, out_ref, log_ref):
    heads, tokens = step_ref.shape
    channels = x_ref.shape[1]
    width = channels // heads
    owner = head_of_channel(heads, channels)
    step = step_ref[...]
    log_cum = log_cumulative(step, as_column(rate_ref[...]))
    log_col = log_cum.T
    mix_in, mix_out = b_ref[...], c_ref[...]
    out_back = ob_ref[...]
    out_back_bf = out_back.astype(bf16)
    stepped = (x_ref[...].astype(f32) * spread(step, owner)).astype(bf16)
    mix_dot = dot(mix_in, mix_out, TN)
    row = lax.broadcasted_iota(jnp.int32, (tokens, tokens), 0)
    col = lax.broadcasted_iota(jnp.int32, (tokens, tokens), 1)
    upper = row <= col
    group_pair = jnp.zeros((tokens, tokens), f32)
    parts, later, earlier = [], [], []
    for h in range(heads):
        gaps = log_cum[h : h + 1, :] - log_col[:, h : h + 1]
        decay = jnp.exp(jnp.where(upper, gaps, -1e30))
        mine = slice(h * width, (h + 1) * width)
        weighted = decay * dot(stepped[:, mine], out_back_bf[:, mine], NT)
        group_pair = group_pair + weighted
        terms = weighted * mix_dot
        later.append(jnp.sum(terms, axis=0, keepdims=True))
        earlier.append(jnp.sum(terms, axis=1, keepdims=True))
        parts.append(dot((decay * mix_dot).astype(bf16), out_back_bf[:, mine]))
    adj_ref[...] = jnp.concatenate(parts, axis=1)
    begin = begin_ref[...]
    decayed = out_back * spread(jnp.exp(log_cum), owner)
    pair_bf = group_pair.astype(bf16)
    in_ref[...] = dot(mix_out, pair_bf, NT)
    out_ref[...] = dot(mix_in, pair_bf) + dot(begin.astype(bf16), decayed.astype(bf16), NT)
    from_state = dot(mix_out.astype(f32), begin, TN)
    net = jnp.concatenate(later, axis=0) - jnp.concatenate(earlier, axis=1).T
    net = net + head_sums(owner, decayed * from_state)
    log_ref[...] = triangle_sums(net, (row >= col).astype(f32))


def scan_pairs(x, out_back, mix_in, mix_out, step, rate, begin):
    length, channels = x.shape
    heads = step.shape[0]
    states = mix_out.shape[1]
    blocks = length // BLOCK
    whole = lambda shape: pl.BlockSpec(shape, lambda b: (0,) * len(shape))
    rows = pl.BlockSpec((BLOCK, channels), lambda b: (b, 0))
    mix = pl.BlockSpec(squeezed(states, BLOCK), lambda b: (0, 0, b))
    line = pl.BlockSpec((heads, BLOCK), lambda b: (0, b))
    return pl.pallas_call(
        pairs_body,
        grid=(blocks,),
        in_specs=[rows, rows, mix, mix, line, whole((1, heads)),
                  pl.BlockSpec(squeezed(states, channels), lambda b: (b, 0, 0))],
        out_specs=[rows, mix, mix, line],
        out_shape=[in_hbm((length, channels), f32),
                   in_hbm((1, states, length), f32),
                   in_hbm((1, states, length), f32),
                   in_hbm((heads, length), f32)],
        compiler_params=limits(28),
        cost_estimate=cost(11),
        name="scan_pairs",
    )(x, out_back, mix_in, mix_out, step, rate, begin)


def finish_body(x_ref, ob_ref, adj_ref, b_ref, step_ref, rate_ref, skip_ref, begin_ref, end_ref,
                in_part_ref, log_part_ref, incoming_ref,
                grad_ref, in_ref, step_grad_ref, carried_ref):
    heads, tokens = step_ref.shape
    channels = x_ref.shape[1]

    @pl.when(pl.program_id(0) == 0)
    def _():
        carried_ref[...] = incoming_ref[...]

    owner = head_of_channel(heads, channels)
    x = x_ref[...].astype(f32)
    step = step_ref[...]
    rate = as_column(rate_ref[...])
    log_cum = log_cumulative(step, rate)
    last = log_cum[:, tokens - 1 :]
    carried = carried_ref[...]
    end = end_ref[...] + carried
    mix_in = b_ref[...]
    end_decay = spread(jnp.exp(last - log_cum), owner)
    stepped = spread(step, owner)
    end_back = dot(mix_in.astype(f32), end, TN) * end_decay
    adjoint = adj_ref[...] + end_back
    grad_ref[...] = (head_row(owner, as_column(skip_ref[...])) * ob_ref[...] + stepped * adjoint).astype(bf16)
    in_ref[...] = in_part_ref[...] + dot(end.astype(bf16), (stepped * end_decay * x).astype(bf16), NT)
    end_term = step * head_sums(owner, x * end_back)
    row = lax.broadcasted_iota(jnp.int32, (tokens, tokens), 0)
    col = lax.broadcasted_iota(jnp.int32, (tokens, tokens), 1)
    block_decay = jnp.exp(last)
    both = jnp.sum(end * begin_ref[...], axis=0, keepdims=True)
    whole_term = block_decay * jnp.sum(owner.astype(f32) * both, axis=1, keepdims=True)
    log_grad = log_part_ref[...] + triangle_sums(end_term, (row < col).astype(f32)) + whole_term
    step_grad_ref[...] = head_sums(owner, x * adjoint) - rate * log_grad
    carried_ref[...] = head_row(owner, block_decay) * carried


def scan_finish(x, out_back, adjoint, mix_in, step, rate, skip, begin, end, in_part, log_part, incoming):
    length, channels = x.shape
    heads = step.shape[0]
    states = mix_in.shape[1]
    blocks = length // BLOCK
    last = blocks - 1
    whole = lambda shape: pl.BlockSpec(shape, lambda b: (0,) * len(shape))
    rows = pl.BlockSpec((BLOCK, channels), lambda b: (last - b, 0))
    mix = pl.BlockSpec(squeezed(states, BLOCK), lambda b: (0, 0, last - b))
    line = pl.BlockSpec((heads, BLOCK), lambda b: (0, last - b))
    state = pl.BlockSpec(squeezed(states, channels), lambda b: (last - b, 0, 0))
    return pl.pallas_call(
        finish_body,
        grid=(blocks,),
        in_specs=[rows, rows, rows, mix, line, whole((1, heads)), whole((1, heads)), state, state,
                  mix, line, whole(incoming.shape)],
        out_specs=[rows, mix, line],
        scratch_shapes=[pltpu.VMEM((states, channels), f32)],
        out_shape=[in_hbm((length, channels), bf16),
                   in_hbm((1, states, length), f32),
                   in_hbm((heads, length), f32)],
        compiler_params=limits(24),
        cost_estimate=cost(9),
        name="scan_finish",
    )(x, out_back, adjoint, mix_in, step, rate, skip, begin, end, in_part, log_part, incoming)


CHUNKS = 8
OFFSETS = (0, -1, 1, 2)


def shifted(value, axis, by):
    size = lax.axis_size(axis)
    return lax.ppermute(value, axis, [(k, (k + by) % size) for k in range(size)])


def swapped(value):
    return shifted(value, "exp_1", 1)


def ring_rest(rows, right, left):
    half = rows.shape[0] // 2
    ahead = shifted(right[:half], "exp_0", 1)
    behind = shifted(left[half:], "exp_0", -1)
    local = [rows, right, left, ahead, behind]
    return local + [swapped(piece) for piece in local]


def ring_pieces(rows):
    return ring_rest(rows, shifted(rows, "exp_0", 1), shifted(rows, "exp_0", -1))


def chunk_index(place_ref, slot):
    chip, core = place_ref[0], place_ref[1]
    return (chip + OFFSETS[slot % 4] + 4) % 4 * 2 + (core + slot // 4) % 2


def chunk_values(refs, slot):
    side, turn = slot // 4 * 5, slot % 4
    if turn < 3:
        return refs[side + turn][...]
    return jnp.concatenate([refs[side + 3][...], refs[side + 4][...]], axis=0)


PARTS = 3
EXTRA = 128


def payload_body(mid_ref, gain_ref, choice_ref, weight_ref, out_ref):
    width = mid_ref.shape[1]
    mid = mid_ref[...].astype(f32)
    scale = lax.rsqrt(jnp.mean(mid * mid, axis=1, keepdims=True) + norm_eps)
    out_ref[:, :width] = (mid * scale * gain_ref[...]).astype(bf16)
    tokens = choice_ref.shape[1]
    lines = jnp.concatenate(
        [choice_ref[...].astype(f32), weight_ref[...], jnp.zeros((4, tokens), f32)], axis=0
    ).T
    lane = lax.broadcasted_iota(jnp.int32, (tokens, EXTRA), 1)
    owner, part = (lane // PARTS).astype(f32), lane % PARTS
    held = jnp.zeros((tokens, EXTRA), f32)
    for k in range(2):
        share = lines[:, 2 + k : 3 + k]
        high = share.astype(bf16).astype(f32)
        middle = (share - high).astype(bf16).astype(f32)
        low = share - high - middle
        value = jnp.where(part == 0, high, jnp.where(part == 1, middle, low))
        held = held + jnp.where(owner == lines[:, k : k + 1], value, 0.0)
    out_ref[:, width:] = held.astype(bf16)


def payload(mid, gain, choice, weight):
    tokens, width = mid.shape
    return pl.pallas_call(
        payload_body,
        out_shape=jax.ShapeDtypeStruct((tokens, width + EXTRA), bf16),
        compiler_params=limits(56),
        cost_estimate=cost(2),
        name="payload",
    )(mid, gain, choice, weight)


def slots_of(share, capacity):
    tokens = share.shape[1]
    hit = share > 0
    row = lax.broadcasted_iota(jnp.int32, (tokens, tokens), 0)
    col = lax.broadcasted_iota(jnp.int32, (tokens, tokens), 1)
    before = dot(hit.astype(f32).astype(bf16), (row < col).astype(f32).astype(bf16))
    rank = jnp.where(hit, before, -1.0)
    place = lax.broadcasted_iota(jnp.int32, (capacity, tokens), 0).astype(f32)
    return [place == rank[slot : slot + 1] for slot in range(share.shape[0])]


def collect_body(place_ref, *refs):
    pieces, extras, out_ref, share_ref = refs[:10], refs[10:20], refs[20], refs[21]
    capacity = out_ref.shape[0] // CHUNKS
    lane = lax.broadcasted_iota(jnp.int32, (8, EXTRA), 1)
    mine = (lane // PARTS == place_ref[0] * 2 + place_ref[1]).astype(f32).astype(bf16)
    share = jnp.concatenate(
        [dot(mine, chunk_values(extras, slot), NT)[:1] for slot in range(CHUNKS)], axis=0
    )
    share_ref[...] = share
    for slot, chosen in enumerate(slots_of(share, capacity)):
        rows = dot(chosen.astype(f32).astype(bf16), chunk_values(pieces, slot))
        out_ref[slot * capacity : (slot + 1) * capacity, :] = rows.astype(bf16)


TILES = 4


def collect(place, pieces, capacity):
    width = pieces[0].shape[1] - EXTRA
    tokens = pieces[0].shape[0]
    tile = width // TILES
    cut = lambda rows: pl.BlockSpec((rows, tile), lambda i, place: (0, i))
    extra = lambda rows: pl.BlockSpec((rows, EXTRA), lambda i, place: (0, width // EXTRA))
    return pl.pallas_call(
        collect_body,
        grid_spec=pltpu.PrefetchScalarGridSpec(
            num_scalar_prefetch=1,
            grid=(TILES,),
            in_specs=[cut(leaf.shape[0]) for leaf in pieces] + [extra(leaf.shape[0]) for leaf in pieces],
            out_specs=[cut(CHUNKS * capacity), pl.BlockSpec((CHUNKS, tokens), lambda i, place: (0, 0))],
        ),
        out_shape=[jax.ShapeDtypeStruct((CHUNKS * capacity, width), bf16),
                   jax.ShapeDtypeStruct((CHUNKS, tokens), f32)],
        compiler_params=limits(16),
        cost_estimate=cost(4),
        name="collect",
    )(place, *pieces, *pieces)


def collect_scaled_body(share_ref, *refs):
    pieces, out_ref = refs[:10], refs[10]
    capacity = out_ref.shape[0] // CHUNKS
    share = share_ref[...]
    for slot, chosen in enumerate(slots_of(share, capacity)):
        rows = dot(chosen.astype(f32).astype(bf16), chunk_values(pieces, slot))
        weight = jnp.sum(jnp.where(chosen, share[slot : slot + 1], 0.0), axis=1, keepdims=True)
        out_ref[slot * capacity : (slot + 1) * capacity, :] = (rows * weight).astype(bf16)


def column_call(body, share, arrays, out_shape, name, micros):
    tile = arrays[0].shape[1] // TILES
    cut = lambda leaf: pl.BlockSpec((leaf.shape[0], tile), lambda i: (0, i))
    return pl.pallas_call(
        body,
        grid=(TILES,),
        in_specs=[pl.BlockSpec(share.shape, lambda i: (0, 0))] + [cut(leaf) for leaf in arrays],
        out_specs=jax.tree.map(cut, out_shape),
        out_shape=out_shape,
        compiler_params=limits(16),
        cost_estimate=cost(micros),
        name=name,
    )(share, *arrays)


def collect_scaled(share, pieces, capacity):
    shape = jax.ShapeDtypeStruct((CHUNKS * capacity, pieces[0].shape[1]), bf16)
    return column_call(collect_scaled_body, share, pieces, shape, "collect_scaled", 4)


def deliver_body(share_ref, rows_ref, *outs):
    capacity = rows_ref.shape[0] // CHUNKS
    for slot, chosen in enumerate(slots_of(share_ref[...], capacity)):
        rows = rows_ref[slot * capacity : (slot + 1) * capacity, :]
        outs[slot][...] = dot(chosen.astype(f32).astype(bf16), rows, TN).astype(bf16)


def deliver(share, rows):
    shape = jax.ShapeDtypeStruct((share.shape[1], rows.shape[1]), bf16)
    return column_call(deliver_body, share, [rows], [shape] * CHUNKS, "deliver", 3)


def returned_sum(parts, done):
    here = [part + swapped(other) for part, other in zip(parts[:4], parts[4:])]
    mine, behind, ahead, across = here
    half = mine.shape[0] // 2
    first = shifted(jnp.concatenate([across[:half], ahead[half:]], axis=0), "exp_0", 1)
    second = shifted(jnp.concatenate([behind[:half], across[half:]], axis=0), "exp_0", -1)
    first, second, _ = lax.optimization_barrier((first, second, done))
    left = shifted(ahead[:half] + first[:half], "exp_0", 1)
    right = shifted(behind[half:] + second[half:], "exp_0", -1)
    wide = lambda part: part.astype(f32)
    return wide(mine) + jnp.concatenate(
        [wide(left) + wide(second[:half]), wide(first[half:]) + wide(right)], axis=0
    )


def out_partials_body(left_ref, right_ref, out_ref, turned_ref):
    width = out_ref.shape[2]

    @pl.when(pl.program_id(0) == 0)
    def _():
        turned_ref[...] = left_ref[...].T

    product = dot(turned_ref[...], right_ref[...]).astype(bf16)
    for k in range(out_ref.shape[0]):
        out_ref[k] = product[:, k * width : (k + 1) * width]


def out_partials(left, right, pieces):
    rows, height = left.shape
    width = right.shape[1] // pieces
    return pl.pallas_call(
        out_partials_body,
        grid=(pieces // 4,),
        in_specs=[pl.BlockSpec((rows, height), lambda i: (0, 0)),
                  pl.BlockSpec((rows, 4 * width), lambda i: (0, i))],
        out_specs=pl.BlockSpec((4, height, width), lambda i: (i, 0, 0)),
        out_shape=in_hbm((pieces, height, width), bf16),
        scratch_shapes=[pltpu.VMEM((height, rows), bf16)],
        compiler_params=limits(24),
        cost_estimate=cost(5),
        name="out_partials",
    )(left, right)


def row_partials_body(in_ref, grad_ref, gate_ref, up_ref, hidden_ref, out_ref):
    width = gate_ref.shape[1]
    turned = in_ref[...].T
    out_ref[:, :width] = dot(turned, gate_ref[...]).astype(bf16)
    out_ref[:, width : 2 * width] = dot(turned, up_ref[...]).astype(bf16)
    out_ref[:, 2 * width :] = dot(grad_ref[...].T, hidden_ref[...]).astype(bf16)


def row_partials(rows_in, rows_grad, gate, up, hidden):
    rows, height = rows_in.shape
    width = gate.shape[1]
    tile = 512
    cut = pl.BlockSpec((rows, tile), lambda i: (0, i))
    whole = pl.BlockSpec((rows, width), lambda i: (0, 0))
    return pl.pallas_call(
        row_partials_body,
        grid=(height // tile,),
        in_specs=[cut, cut, whole, whole, whole],
        out_specs=pl.BlockSpec((tile, 3 * width), lambda i: (i, 0)),
        out_shape=in_hbm((height, 3 * width), bf16),
        compiler_params=limits(32),
        cost_estimate=cost(9),
        name="row_partials",
    )(rows_in, rows_grad, gate, up, hidden)


def row_of(joined):
    joined = joined.astype(f32)
    return joined[:-1], joined[-1:]


def incoming_adjoint(joined):
    size = lax.axis_size("seq")
    side = 4
    mine = lax.axis_index("seq")
    column, row = mine % side, mine // side

    def from_column(value, by):
        return lax.ppermute(
            value, "seq", [(k // side * side + (k + by) % side, k) for k in range(size)])

    def from_row(value, by):
        return lax.ppermute(value, "seq", [((k + by * side) % size, k) for k in range(size)])

    adjoint, decay = row_of(joined)
    others = [row_of(from_column(joined, by)) for by in range(1, side)]
    after, reach = jnp.zeros_like(adjoint), jnp.ones_like(decay)
    for by in range(side - 1, 0, -1):
        there, fade = others[by - 1]
        valid = column + by < side
        after = jnp.where(valid, there + fade * after, after)
        reach = jnp.where(valid, fade * reach, reach)
    total, whole = adjoint + decay * after, decay
    for by in range(side - 1, 0, -1):
        there, fade = others[by - 1]
        total = jnp.where(column + by >= side, there + fade * total, total)
        whole = whole * fade
    sent = jnp.concatenate([total, whole], axis=0).astype(bf16)
    rows = [row_of(from_row(sent, by)) for by in range(1, size // side)]
    beyond = jnp.zeros_like(adjoint)
    for by in range(size // side - 1, 0, -1):
        there, fade = rows[by - 1]
        beyond = jnp.where(row + by < size // side, there + fade * beyond, beyond)
    return after + reach * beyond


def shards(
    scan_input,
    gate_input,
    input_mix,
    output_mix,
    step_size,
    decay_rate,
    skip_scale,
    norm_gain,
    entry_state,
    out_weight,
    block_mid,
    expert_gain,
    expert_choice,
    route_weight,
    gate_proj,
    up_proj,
    down_proj,
    out_grad,
):
    channels = scan_input.shape[1]
    heads = step_size.shape[0]
    states = input_mix.shape[1]
    experts = lax.axis_size(EXP)
    ranges = lax.axis_size("seq")
    tokens = block_mid.shape[0]
    capacity = 4 * tokens // experts
    place = jnp.stack([lax.axis_index(axis) for axis in ("exp_0", "exp_1", "seq")]).astype(jnp.int32)
    rate, skip, gain = decay_rate[None], skip_scale[None], norm_gain[None]

    mid_values = block_mid.astype(f32)
    mid_scale = lax.rsqrt(jnp.mean(mid_values * mid_values, axis=1, keepdims=True) + norm_eps)
    tokens_out = payload(block_mid, expert_gain[None], expert_choice.T, route_weight.T)
    near = (shifted(tokens_out, "exp_0", 1), shifted(tokens_out, "exp_0", -1))

    y, normed, begin = scan_forward(
        scan_input, gate_input, input_mix, output_mix, step_size, rate, skip, gain,
        entry_state.reshape(channels, states),
    )
    near, y, grads_out = lax.optimization_barrier((near, y, out_grad))
    in_pieces = ring_rest(tokens_out, *near)
    grad_pieces = ring_pieces(grads_out)

    gate_matrix, up_matrix, down_matrix = gate_proj[0], up_proj[0], down_proj[0]
    rows_in, share = collect(place, in_pieces, capacity)
    gate_pre = dot(rows_in, gate_matrix)
    up_pre = dot(rows_in, up_matrix)
    grad_pieces, up_pre = lax.optimization_barrier((grad_pieces, up_pre))
    rows_grad = collect_scaled(share, grad_pieces, capacity)
    hidden_back = dot(rows_grad, down_matrix, NT)
    gate_act, gate_slope = silu_parts(gate_pre)
    hidden = (gate_act * up_pre).astype(bf16)
    gate_back = (hidden_back * up_pre * gate_slope).astype(bf16)
    up_back = (hidden_back * gate_act).astype(bf16)
    partials = row_partials(rows_in, rows_grad, gate_back, up_back, hidden)
    gate_back, up_back, partials = lax.optimization_barrier((gate_back, up_back, partials))
    rows_back = dot(gate_back, gate_matrix, NT) + dot(up_back, up_matrix, NT)
    parts = deliver(share, rows_back.astype(bf16))
    summed = lax.psum_scatter(partials, "seq", scatter_dimension=0, tiled=True)

    weighted_back = returned_sum(parts, partials) * expert_gain
    mid_grad = (
        out_grad.astype(f32)
        + mid_scale * weighted_back
        - mid_values * mid_scale**3 * jnp.mean(mid_values * weighted_back, axis=1, keepdims=True)
    ).astype(bf16)
    out_back, gate_grad, end, joined, shard_rows = scan_backward(
        place, ring_pieces(mid_grad), out_weight, y, gate_input, output_mix, step_size, rate, gain
    )
    incoming = incoming_adjoint(joined)
    out_parts = lax.all_to_all(out_partials(normed, shard_rows, ranges), "seq", 0, 0, tiled=True)
    inner, in_part, out_mix_grad, log_part = scan_pairs(
        scan_input, out_back, input_mix, output_mix, step_size, rate, begin
    )
    input_grad, in_mix_grad, step_grad = scan_finish(
        scan_input, out_back, inner, input_mix, step_size, rate, skip, begin, end,
        in_part, log_part, incoming,
    )
    width = gate_back.shape[1]
    summed = summed.astype(f32)
    return (
        mid_grad,
        input_grad,
        gate_grad,
        in_mix_grad,
        out_mix_grad,
        step_grad,
        jnp.sum(out_parts.astype(f32), axis=0),
        summed[None, :, :width],
        summed[None, :, width : 2 * width],
        summed[None, :, 2 * width :].transpose(0, 2, 1),
    )


def solution(mesh):
    split = Mesh(mesh.devices.reshape(mesh.shape["seq"], 4, 2), ("seq", "exp_0", "exp_1"))
    placed = (
        P("seq", EXP),
        P("seq", EXP),
        P(EXP, None, "seq"),
        P(EXP, None, "seq"),
        P(EXP, "seq"),
        P(EXP),
        P(EXP),
        P(EXP),
        P("seq", EXP, None, None),
        P(EXP, None),
        P(SEQ_EXP, None),
        P(),
        P(SEQ_EXP, None),
        P(SEQ_EXP, None),
        P(EXP, None, None),
        P(EXP, None, None),
        P(EXP, None, None),
        P(SEQ_EXP, None),
    )
    return jax.shard_map(
        shards,
        mesh=split,
        in_specs=placed,
        out_specs=(
            P(SEQ_EXP, None),
            P("seq", EXP),
            P("seq", EXP),
            P(EXP, None, "seq"),
            P(EXP, None, "seq"),
            P(EXP, "seq"),
            P(EXP, "seq"),
            P(EXP, "seq", None),
            P(EXP, "seq", None),
            P(EXP, None, "seq"),
        ),
        check_vma=False,
    )
```

```python
import jax
import jax.numpy as jnp
from jax import lax
from jax.experimental import pallas as pl
from jax.experimental.pallas import tpu as pltpu
from jax.sharding import Mesh
from jax.sharding import PartitionSpec as P

BLOCK = 256
EXP = ("exp_0", "exp_1")
SEQ_EXP = ("seq", "exp_0", "exp_1")
norm_eps = 1e-05
f32 = jnp.float32
bf16 = jnp.bfloat16


def dot(a, b, dims=((1,), (0,)), precision=None):
    return lax.dot_general(a, b, (dims, ((), ())), preferred_element_type=f32, precision=precision)


NT = ((1,), (1,))
TN = ((0,), (0,))


def split_two(value):
    high = value.astype(bf16)
    return high, (value - high.astype(f32)).astype(bf16)


def head_of_channel(heads, channels):
    row = lax.broadcasted_iota(jnp.int32, (heads, channels), 0)
    col = lax.broadcasted_iota(jnp.int32, (heads, channels), 1)
    return (col // (channels // heads) == row).astype(bf16)


def spread(per_head, owner):
    high, low = split_two(per_head)
    return dot(high, owner, TN) + dot(low, owner, TN)


def head_sums(owner, value):
    high, low = split_two(value)
    return dot(owner, high, NT) + dot(owner, low, NT)


def as_column(row):
    size = row.shape[1]
    same = lax.broadcasted_iota(jnp.int32, (size, size), 0) == lax.broadcasted_iota(jnp.int32, (size, size), 1)
    return jnp.sum(jnp.where(same, row, 0.0), axis=1, keepdims=True)


def in_hbm(shape, kind):
    return pltpu.HBM(shape, kind)


def limits(mib):
    return pltpu.CompilerParams(vmem_limit_bytes=mib << 20)


def cost(micros):
    return pl.CostEstimate(flops=int(micros * 9e8), transcendentals=0, bytes_accessed=int(micros * 2e6))


def head_row(owner, column):
    return jnp.sum(owner.astype(f32) * column, axis=0, keepdims=True)


def triangle_sums(rows, triangle):
    count = rows.shape[0]
    high, rest = rows.astype(bf16), rows - rows.astype(bf16).astype(f32)
    middle, low = split_two(rest)
    three = dot(jnp.concatenate([high.astype(f32), middle.astype(f32), low.astype(f32)], axis=0).astype(bf16),
                triangle.astype(bf16))
    return three[:count] + three[count : 2 * count] + three[2 * count :]


def log_cumulative(step, rate):
    tokens = step.shape[1]
    row = lax.broadcasted_iota(jnp.int32, (tokens, tokens), 0)
    col = lax.broadcasted_iota(jnp.int32, (tokens, tokens), 1)
    return triangle_sums(-step * rate, (row <= col).astype(f32))


def silu_parts(values):
    sigmoid = 1.0 / (1.0 + jnp.exp(-values))
    return values * sigmoid, sigmoid * (1.0 + values * (1.0 - sigmoid))


def forward_body(x_ref, z_ref, b_ref, c_ref, step_ref, rate_ref, skip_ref, gain_ref, entry_ref,
                 y_ref, normed_ref, begin_ref, state_ref):
    heads, tokens = step_ref.shape
    channels = x_ref.shape[1]
    width = channels // heads

    @pl.when(pl.program_id(0) == 0)
    def _():
        state_ref[...] = entry_ref[...].T

    owner = head_of_channel(heads, channels)
    x = x_ref[...].astype(f32)
    step = step_ref[...]
    log_cum = log_cumulative(step, as_column(rate_ref[...]))
    log_col = log_cum.T
    mix_in, mix_out = b_ref[...], c_ref[...]
    stepped = x * spread(step, owner)
    stepped_bf = stepped.astype(bf16)
    mix_dot = dot(mix_out, mix_in, TN)
    row = lax.broadcasted_iota(jnp.int32, (tokens, tokens), 0)
    col = lax.broadcasted_iota(jnp.int32, (tokens, tokens), 1)
    lower = row >= col
    parts = []
    for h in range(heads):
        gaps = log_col[:, h : h + 1] - log_cum[h : h + 1, :]
        kernel = (jnp.exp(jnp.where(lower, gaps, -1e30)) * mix_dot).astype(bf16)
        parts.append(dot(kernel, stepped_bf[:, h * width : (h + 1) * width]))
    state = state_ref[...]
    begin_ref[...] = state
    from_state = dot(mix_out.astype(f32), state, TN) * spread(jnp.exp(log_cum), owner)
    y = jnp.concatenate(parts, axis=1) + from_state + head_row(owner, as_column(skip_ref[...])) * x
    y_ref[...] = y
    last = log_cum[:, tokens - 1 :]
    ended = (stepped * spread(jnp.exp(last - log_cum), owner)).astype(bf16)
    state_ref[...] = head_row(owner, jnp.exp(last)) * state + dot(mix_in, ended)
    gate_act, _ = silu_parts(z_ref[...].astype(f32))
    gated = y * gate_act
    scale = lax.rsqrt(jnp.mean(gated * gated, axis=1, keepdims=True) + norm_eps)
    normed_ref[...] = (gated * scale * gain_ref[...]).astype(bf16)


def squeezed(*shape):
    return (pl.Squeezed(), *shape)


def scan_forward(x, z, mix_in, mix_out, step, rate, skip, gain, entry):
    length, channels = x.shape
    heads = step.shape[0]
    states = mix_in.shape[1]
    blocks = length // BLOCK
    whole = lambda shape: pl.BlockSpec(shape, lambda b: (0,) * len(shape))
    rows = pl.BlockSpec((BLOCK, channels), lambda b: (b, 0))
    mix = pl.BlockSpec(squeezed(states, BLOCK), lambda b: (0, 0, b))
    return pl.pallas_call(
        forward_body,
        grid=(blocks,),
        in_specs=[rows, rows, mix, mix, pl.BlockSpec((heads, BLOCK), lambda b: (0, b)),
                  whole((1, heads)), whole((1, heads)), whole((1, channels)), whole((channels, states))],
        out_specs=[rows, rows, pl.BlockSpec(squeezed(states, channels), lambda b: (b, 0, 0))],
        out_shape=[in_hbm((length, channels), f32),
                   in_hbm((length, channels), bf16),
                   in_hbm((blocks, states, channels), f32)],
        scratch_shapes=[pltpu.VMEM((states, channels), f32)],
        compiler_params=limits(24),
        cost_estimate=cost(9),
        name="scan_forward",
    )(x, z, mix_in, mix_out, step, rate, skip, gain, entry)


def backward_body(place_ref, *refs):
    pieces = refs[:10]
    (weight_ref, y_ref, z_ref, c_ref, step_ref, rate_ref, gain_ref,
     out_back_ref, gate_grad_ref, end_ref, joined_ref, rows_ref, state_ref, decay_ref, all_ref) = refs[10:]
    heads, tokens = step_ref.shape
    channels = y_ref.shape[1]
    states = state_ref.shape[0]

    @pl.when(pl.program_id(0) == 0)
    def _():
        state_ref[...] = jnp.zeros_like(state_ref)
        decay_ref[...] = jnp.ones_like(decay_ref)
        count = pieces[0].shape[0]
        half = count // 2
        for side in range(2):
            for turn in range(5):
                start = chunk_index(place_ref, side * 4 + min(turn, 3)) * count + (half if turn == 4 else 0)
                piece = pieces[side * 5 + turn]
                all_ref[pl.ds(pl.multiple_of(start, half), piece.shape[0]), :] = piece[...]

    owner = head_of_channel(heads, channels)
    log_cum = log_cumulative(step_ref[...], as_column(rate_ref[...]))
    block = pl.num_programs(0) - 1 - pl.program_id(0)
    rows = all_ref[pl.ds(pl.multiple_of(block * tokens, tokens), tokens), :]
    rows_ref[...] = rows
    projected = dot(rows, weight_ref[...], NT)
    y = y_ref[...]
    gate_act, gate_slope = silu_parts(z_ref[...].astype(f32))
    gated = y * gate_act
    scale = lax.rsqrt(jnp.mean(gated * gated, axis=1, keepdims=True) + norm_eps)
    scaled = projected * gain_ref[...]
    inner = jnp.mean(gated * scaled, axis=1, keepdims=True)
    gated_back = scale * scaled - gated * (scale * scale * scale * inner)
    out_back = gated_back * gate_act
    gate_grad_ref[...] = (gated_back * y * gate_slope).astype(bf16)
    out_back_ref[...] = out_back
    state = state_ref[...]
    end_ref[...] = state
    decayed = (out_back * spread(jnp.exp(log_cum), owner)).astype(bf16)
    block_decay = head_row(owner, jnp.exp(log_cum[:, tokens - 1 :]))
    state = block_decay * state + dot(c_ref[...], decayed)
    decay = block_decay * decay_ref[...]
    state_ref[...] = state
    decay_ref[...] = decay
    joined_ref[:states, :] = state.astype(bf16)
    joined_ref[states:, :] = decay.astype(bf16)


def scan_backward(place, pieces, weight, y, z, mix_out, step, rate, gain):
    length, channels = y.shape
    heads = step.shape[0]
    states = mix_out.shape[1]
    blocks = length // BLOCK
    last = blocks - 1
    width = weight.shape[1]
    whole = lambda shape: pl.BlockSpec(shape, lambda b, place: (0,) * len(shape))
    rows = pl.BlockSpec((BLOCK, channels), lambda b, place: (last - b, 0))
    mix = pl.BlockSpec(squeezed(states, BLOCK), lambda b, place: (0, 0, last - b))
    return pl.pallas_call(
        backward_body,
        grid_spec=pltpu.PrefetchScalarGridSpec(
            num_scalar_prefetch=1,
            grid=(blocks,),
            in_specs=[whole(piece.shape) for piece in pieces] + [
                whole(weight.shape), rows, rows, mix,
                pl.BlockSpec((heads, BLOCK), lambda b, place: (0, last - b)),
                whole((1, heads)), whole((1, channels))],
            out_specs=[rows, rows, pl.BlockSpec(squeezed(states, channels), lambda b, place: (last - b, 0, 0)),
                       whole((states + 1, channels)),
                       pl.BlockSpec((BLOCK, width), lambda b, place: (last - b, 0))],
            scratch_shapes=[pltpu.VMEM((states, channels), f32), pltpu.VMEM((1, channels), f32),
                            pltpu.VMEM((length, width), bf16)],
        ),
        out_shape=[in_hbm((length, channels), f32),
                   in_hbm((length, channels), bf16),
                   in_hbm((blocks, states, channels), f32),
                   in_hbm((states + 1, channels), bf16),
                   in_hbm((length, width), bf16)],
        compiler_params=limits(56),
        cost_estimate=cost(9),
        name="scan_backward",
    )(place, *pieces, weight, y, z, mix_out, step, rate, gain)


def pairs_body(x_ref, ob_ref, b_ref, c_ref, step_ref, rate_ref, begin_ref,
               adj_ref, in_ref, out_ref, log_ref):
    heads, tokens = step_ref.shape
    channels = x_ref.shape[1]
    width = channels // heads
    owner = head_of_channel(heads, channels)
    step = step_ref[...]
    log_cum = log_cumulative(step, as_column(rate_ref[...]))
    log_col = log_cum.T
    mix_in, mix_out = b_ref[...], c_ref[...]
    out_back = ob_ref[...]
    out_back_bf = out_back.astype(bf16)
    stepped = (x_ref[...].astype(f32) * spread(step, owner)).astype(bf16)
    mix_dot = dot(mix_in, mix_out, TN)
    row = lax.broadcasted_iota(jnp.int32, (tokens, tokens), 0)
    col = lax.broadcasted_iota(jnp.int32, (tokens, tokens), 1)
    upper = row <= col
    group_pair = jnp.zeros((tokens, tokens), f32)
    parts, later, earlier = [], [], []
    for h in range(heads):
        gaps = log_cum[h : h + 1, :] - log_col[:, h : h + 1]
        decay = jnp.exp(jnp.where(upper, gaps, -1e30))
        mine = slice(h * width, (h + 1) * width)
        weighted = decay * dot(stepped[:, mine], out_back_bf[:, mine], NT)
        group_pair = group_pair + weighted
        terms = weighted * mix_dot
        later.append(jnp.sum(terms, axis=0, keepdims=True))
        earlier.append(jnp.sum(terms, axis=1, keepdims=True))
        parts.append(dot((decay * mix_dot).astype(bf16), out_back_bf[:, mine]))
    adj_ref[...] = jnp.concatenate(parts, axis=1)
    begin = begin_ref[...]
    decayed = out_back * spread(jnp.exp(log_cum), owner)
    pair_bf = group_pair.astype(bf16)
    in_ref[...] = dot(mix_out, pair_bf, NT)
    out_ref[...] = dot(mix_in, pair_bf) + dot(begin.astype(bf16), decayed.astype(bf16), NT)
    from_state = dot(mix_out.astype(f32), begin, TN)
    net = jnp.concatenate(later, axis=0) - jnp.concatenate(earlier, axis=1).T
    net = net + head_sums(owner, decayed * from_state)
    log_ref[...] = triangle_sums(net, (row >= col).astype(f32))


def scan_pairs(x, out_back, mix_in, mix_out, step, rate, begin):
    length, channels = x.shape
    heads = step.shape[0]
    states = mix_out.shape[1]
    blocks = length // BLOCK
    whole = lambda shape: pl.BlockSpec(shape, lambda b: (0,) * len(shape))
    rows = pl.BlockSpec((BLOCK, channels), lambda b: (b, 0))
    mix = pl.BlockSpec(squeezed(states, BLOCK), lambda b: (0, 0, b))
    line = pl.BlockSpec((heads, BLOCK), lambda b: (0, b))
    return pl.pallas_call(
        pairs_body,
        grid=(blocks,),
        in_specs=[rows, rows, mix, mix, line, whole((1, heads)),
                  pl.BlockSpec(squeezed(states, channels), lambda b: (b, 0, 0))],
        out_specs=[rows, mix, mix, line],
        out_shape=[in_hbm((length, channels), f32),
                   in_hbm((1, states, length), f32),
                   in_hbm((1, states, length), f32),
                   in_hbm((heads, length), f32)],
        compiler_params=limits(56),
        cost_estimate=cost(11),
        name="scan_pairs",
    )(x, out_back, mix_in, mix_out, step, rate, begin)


def finish_body(x_ref, ob_ref, adj_ref, b_ref, step_ref, rate_ref, skip_ref, begin_ref, end_ref,
                in_part_ref, log_part_ref, incoming_ref,
                grad_ref, in_ref, step_grad_ref, carried_ref):
    heads, tokens = step_ref.shape
    channels = x_ref.shape[1]

    @pl.when(pl.program_id(0) == 0)
    def _():
        carried_ref[...] = incoming_ref[...]

    owner = head_of_channel(heads, channels)
    x = x_ref[...].astype(f32)
    step = step_ref[...]
    rate = as_column(rate_ref[...])
    log_cum = log_cumulative(step, rate)
    last = log_cum[:, tokens - 1 :]
    carried = carried_ref[...]
    end = end_ref[...] + carried
    mix_in = b_ref[...]
    end_decay = spread(jnp.exp(last - log_cum), owner)
    stepped = spread(step, owner)
    end_back = dot(mix_in.astype(f32), end, TN) * end_decay
    adjoint = adj_ref[...] + end_back
    grad_ref[...] = (head_row(owner, as_column(skip_ref[...])) * ob_ref[...] + stepped * adjoint).astype(bf16)
    in_ref[...] = in_part_ref[...] + dot(end.astype(bf16), (stepped * end_decay * x).astype(bf16), NT)
    end_term = step * head_sums(owner, x * end_back)
    row = lax.broadcasted_iota(jnp.int32, (tokens, tokens), 0)
    col = lax.broadcasted_iota(jnp.int32, (tokens, tokens), 1)
    block_decay = jnp.exp(last)
    both = jnp.sum(end * begin_ref[...], axis=0, keepdims=True)
    whole_term = block_decay * jnp.sum(owner.astype(f32) * both, axis=1, keepdims=True)
    log_grad = log_part_ref[...] + triangle_sums(end_term, (row < col).astype(f32)) + whole_term
    step_grad_ref[...] = head_sums(owner, x * adjoint) - rate * log_grad
    carried_ref[...] = head_row(owner, block_decay) * carried


def scan_finish(x, out_back, adjoint, mix_in, step, rate, skip, begin, end, in_part, log_part, incoming):
    length, channels = x.shape
    heads = step.shape[0]
    states = mix_in.shape[1]
    blocks = length // BLOCK
    last = blocks - 1
    whole = lambda shape: pl.BlockSpec(shape, lambda b: (0,) * len(shape))
    rows = pl.BlockSpec((BLOCK, channels), lambda b: (last - b, 0))
    mix = pl.BlockSpec(squeezed(states, BLOCK), lambda b: (0, 0, last - b))
    line = pl.BlockSpec((heads, BLOCK), lambda b: (0, last - b))
    state = pl.BlockSpec(squeezed(states, channels), lambda b: (last - b, 0, 0))
    return pl.pallas_call(
        finish_body,
        grid=(blocks,),
        in_specs=[rows, rows, rows, mix, line, whole((1, heads)), whole((1, heads)), state, state,
                  mix, line, whole(incoming.shape)],
        out_specs=[rows, mix, line],
        scratch_shapes=[pltpu.VMEM((states, channels), f32)],
        out_shape=[in_hbm((length, channels), bf16),
                   in_hbm((1, states, length), f32),
                   in_hbm((heads, length), f32)],
        compiler_params=limits(56),
        cost_estimate=cost(9),
        name="scan_finish",
    )(x, out_back, adjoint, mix_in, step, rate, skip, begin, end, in_part, log_part, incoming)


CHUNKS = 8
OFFSETS = (0, -1, 1, 2)


def shifted(value, axis, by):
    size = lax.axis_size(axis)
    return lax.ppermute(value, axis, [(k, (k + by) % size) for k in range(size)])


def swapped(value):
    return shifted(value, "exp_1", 1)


def ring_rest(rows, right, left):
    half = rows.shape[0] // 2
    ahead = shifted(right[:half], "exp_0", 1)
    behind = shifted(left[half:], "exp_0", -1)
    local = [rows, right, left, ahead, behind]
    return local + [swapped(piece) for piece in local]


def ring_pieces(rows):
    return ring_rest(rows, shifted(rows, "exp_0", 1), shifted(rows, "exp_0", -1))


def chunk_index(place_ref, slot):
    chip, core = place_ref[0], place_ref[1]
    return (chip + OFFSETS[slot % 4] + 4) % 4 * 2 + (core + slot // 4) % 2


def chunk_values(refs, slot):
    side, turn = slot // 4 * 5, slot % 4
    if turn < 3:
        return refs[side + turn][...]
    return jnp.concatenate([refs[side + 3][...], refs[side + 4][...]], axis=0)


PARTS = 3
EXTRA = 128


def payload_body(mid_ref, gain_ref, choice_ref, weight_ref, out_ref):
    width = mid_ref.shape[1]
    mid = mid_ref[...].astype(f32)
    scale = lax.rsqrt(jnp.mean(mid * mid, axis=1, keepdims=True) + norm_eps)
    out_ref[:, :width] = (mid * scale * gain_ref[...]).astype(bf16)
    tokens = choice_ref.shape[1]
    lines = jnp.concatenate(
        [choice_ref[...].astype(f32), weight_ref[...], jnp.zeros((4, tokens), f32)], axis=0
    ).T
    lane = lax.broadcasted_iota(jnp.int32, (tokens, EXTRA), 1)
    owner, part = (lane // PARTS).astype(f32), lane % PARTS
    held = jnp.zeros((tokens, EXTRA), f32)
    for k in range(2):
        share = lines[:, 2 + k : 3 + k]
        high = share.astype(bf16).astype(f32)
        middle = (share - high).astype(bf16).astype(f32)
        low = share - high - middle
        value = jnp.where(part == 0, high, jnp.where(part == 1, middle, low))
        held = held + jnp.where(owner == lines[:, k : k + 1], value, 0.0)
    out_ref[:, width:] = held.astype(bf16)


def payload(mid, gain, choice, weight):
    tokens, width = mid.shape
    return pl.pallas_call(
        payload_body,
        out_shape=jax.ShapeDtypeStruct((tokens, width + EXTRA), bf16),
        compiler_params=limits(56),
        cost_estimate=cost(2),
        name="payload",
    )(mid, gain, choice, weight)


def slots_of(share, capacity):
    tokens = share.shape[1]
    hit = share > 0
    row = lax.broadcasted_iota(jnp.int32, (tokens, tokens), 0)
    col = lax.broadcasted_iota(jnp.int32, (tokens, tokens), 1)
    before = dot(hit.astype(f32).astype(bf16), (row < col).astype(f32).astype(bf16))
    rank = jnp.where(hit, before, -1.0)
    place = lax.broadcasted_iota(jnp.int32, (capacity, tokens), 0).astype(f32)
    return [place == rank[slot : slot + 1] for slot in range(share.shape[0])]


def collect_body(place_ref, *refs):
    pieces, extras, out_ref, share_ref = refs[:10], refs[10:20], refs[20], refs[21]
    capacity = out_ref.shape[0] // CHUNKS
    lane = lax.broadcasted_iota(jnp.int32, (8, EXTRA), 1)
    mine = (lane // PARTS == place_ref[0] * 2 + place_ref[1]).astype(f32).astype(bf16)
    share = jnp.concatenate(
        [dot(mine, chunk_values(extras, slot), NT)[:1] for slot in range(CHUNKS)], axis=0
    )
    share_ref[...] = share
    for slot, chosen in enumerate(slots_of(share, capacity)):
        rows = dot(chosen.astype(f32).astype(bf16), chunk_values(pieces, slot))
        out_ref[slot * capacity : (slot + 1) * capacity, :] = rows.astype(bf16)


TILES = 4


def collect(place, pieces, capacity):
    width = pieces[0].shape[1] - EXTRA
    tokens = pieces[0].shape[0]
    tile = width // TILES
    cut = lambda rows: pl.BlockSpec((rows, tile), lambda i, place: (0, i))
    extra = lambda rows: pl.BlockSpec((rows, EXTRA), lambda i, place: (0, width // EXTRA))
    return pl.pallas_call(
        collect_body,
        grid_spec=pltpu.PrefetchScalarGridSpec(
            num_scalar_prefetch=1,
            grid=(TILES,),
            in_specs=[cut(leaf.shape[0]) for leaf in pieces] + [extra(leaf.shape[0]) for leaf in pieces],
            out_specs=[cut(CHUNKS * capacity), pl.BlockSpec((CHUNKS, tokens), lambda i, place: (0, 0))],
        ),
        out_shape=[jax.ShapeDtypeStruct((CHUNKS * capacity, width), bf16),
                   jax.ShapeDtypeStruct((CHUNKS, tokens), f32)],
        compiler_params=limits(16),
        cost_estimate=cost(4),
        name="collect",
    )(place, *pieces, *pieces)


def collect_scaled_body(share_ref, *refs):
    pieces, out_ref = refs[:10], refs[10]
    capacity = out_ref.shape[0] // CHUNKS
    share = share_ref[...]
    for slot, chosen in enumerate(slots_of(share, capacity)):
        rows = dot(chosen.astype(f32).astype(bf16), chunk_values(pieces, slot))
        weight = jnp.sum(jnp.where(chosen, share[slot : slot + 1], 0.0), axis=1, keepdims=True)
        out_ref[slot * capacity : (slot + 1) * capacity, :] = (rows * weight).astype(bf16)


def column_call(body, share, arrays, out_shape, micros):
    tile = arrays[0].shape[1] // TILES
    cut = lambda leaf: pl.BlockSpec((leaf.shape[0], tile), lambda i: (0, i))
    return pl.pallas_call(
        body,
        grid=(TILES,),
        in_specs=[pl.BlockSpec(share.shape, lambda i: (0, 0))] + [cut(leaf) for leaf in arrays],
        out_specs=jax.tree.map(cut, out_shape),
        out_shape=out_shape,
        compiler_params=limits(16),
        cost_estimate=cost(micros),
    )(share, *arrays)


def collect_scaled(share, pieces, capacity):
    shape = jax.ShapeDtypeStruct((CHUNKS * capacity, pieces[0].shape[1]), bf16)
    return column_call(collect_scaled_body, share, pieces, shape, 4)


def deliver_body(share_ref, rows_ref, *outs):
    capacity = rows_ref.shape[0] // CHUNKS
    for slot, chosen in enumerate(slots_of(share_ref[...], capacity)):
        rows = rows_ref[slot * capacity : (slot + 1) * capacity, :]
        outs[slot][...] = dot(chosen.astype(f32).astype(bf16), rows, TN).astype(bf16)


def deliver(share, rows):
    shape = jax.ShapeDtypeStruct((share.shape[1], rows.shape[1]), bf16)
    return column_call(deliver_body, share, [rows], [shape] * CHUNKS, 3)


def returned_sum(parts):
    here = [part + swapped(other) for part, other in zip(parts[:4], parts[4:])]
    mine, behind, ahead, across = here
    half = mine.shape[0] // 2
    first = shifted(jnp.concatenate([across[:half], ahead[half:]], axis=0), "exp_0", 1)
    second = shifted(jnp.concatenate([behind[:half], across[half:]], axis=0), "exp_0", -1)
    left = shifted(ahead[:half] + first[:half], "exp_0", 1)
    right = shifted(behind[half:] + second[half:], "exp_0", -1)
    wide = lambda part: part.astype(f32)
    return wide(mine) + jnp.concatenate(
        [wide(left) + wide(second[:half]), wide(first[half:]) + wide(right)], axis=0
    )


def out_partials_body(left_ref, right_ref, out_ref, turned_ref):
    width = out_ref.shape[2]

    @pl.when(pl.program_id(0) == 0)
    def _():
        turned_ref[...] = left_ref[...].T

    product = dot(turned_ref[...], right_ref[...]).astype(bf16)
    for k in range(out_ref.shape[0]):
        out_ref[k] = product[:, k * width : (k + 1) * width]


def out_partials(left, right, pieces):
    rows, height = left.shape
    width = right.shape[1] // pieces
    return pl.pallas_call(
        out_partials_body,
        grid=(pieces // 4,),
        in_specs=[pl.BlockSpec((rows, height), lambda i: (0, 0)),
                  pl.BlockSpec((rows, 4 * width), lambda i: (0, i))],
        out_specs=pl.BlockSpec((4, height, width), lambda i: (i, 0, 0)),
        out_shape=in_hbm((pieces, height, width), bf16),
        scratch_shapes=[pltpu.VMEM((height, rows), bf16)],
        compiler_params=limits(24),
        cost_estimate=cost(5),
        name="out_partials",
    )(left, right)


def row_partials_body(in_ref, grad_ref, gate_ref, up_ref, hidden_ref, out_ref):
    width = gate_ref.shape[1]
    turned = in_ref[...].T
    out_ref[:, :width] = dot(turned, gate_ref[...]).astype(bf16)
    out_ref[:, width : 2 * width] = dot(turned, up_ref[...]).astype(bf16)
    out_ref[:, 2 * width :] = dot(grad_ref[...].T, hidden_ref[...]).astype(bf16)


def row_partials(rows_in, rows_grad, gate, up, hidden):
    rows, height = rows_in.shape
    width = gate.shape[1]
    tile = 512
    cut = pl.BlockSpec((rows, tile), lambda i: (0, i))
    whole = pl.BlockSpec((rows, width), lambda i: (0, 0))
    return pl.pallas_call(
        row_partials_body,
        grid=(height // tile,),
        in_specs=[cut, cut, whole, whole, whole],
        out_specs=pl.BlockSpec((tile, 3 * width), lambda i: (i, 0)),
        out_shape=in_hbm((height, 3 * width), bf16),
        compiler_params=limits(32),
        cost_estimate=cost(9),
        name="row_partials",
    )(rows_in, rows_grad, gate, up, hidden)


def row_of(joined):
    joined = joined.astype(f32)
    return joined[:-1], joined[-1:]


def incoming_adjoint(joined):
    size = lax.axis_size("seq")
    side = 4
    mine = lax.axis_index("seq")
    column, row = mine % side, mine // side

    def from_column(value, by):
        return lax.ppermute(
            value, "seq", [(k // side * side + (k + by) % side, k) for k in range(size)])

    def from_row(value, by):
        return lax.ppermute(value, "seq", [((k + by * side) % size, k) for k in range(size)])

    adjoint, decay = row_of(joined)
    others = [row_of(from_column(joined, by)) for by in range(1, side)]
    after, reach = jnp.zeros_like(adjoint), jnp.ones_like(decay)
    for by in range(side - 1, 0, -1):
        there, fade = others[by - 1]
        valid = column + by < side
        after = jnp.where(valid, there + fade * after, after)
        reach = jnp.where(valid, fade * reach, reach)
    total, whole = adjoint + decay * after, decay
    for by in range(side - 1, 0, -1):
        there, fade = others[by - 1]
        total = jnp.where(column + by >= side, there + fade * total, total)
        whole = whole * fade
    sent = jnp.concatenate([total, whole], axis=0).astype(bf16)
    rows = [from_row(sent, by) for by in range(1, size // side)]
    rows = [row_of(value) for value in rows]
    beyond = jnp.zeros_like(adjoint)
    for by in range(size // side - 1, 0, -1):
        there, fade = rows[by - 1]
        beyond = jnp.where(row + by < size // side, there + fade * beyond, beyond)
    return after + reach * beyond


def split_sums_body(sum_ref, gate_ref, up_ref, down_ref):
    width = gate_ref.shape[1]
    gate_ref[...] = sum_ref[:, :width].astype(f32)
    up_ref[...] = sum_ref[:, width : 2 * width].astype(f32)
    down_ref[...] = sum_ref[:, 2 * width :].astype(f32).T


def split_sums(summed):
    rows, width = summed.shape[0], summed.shape[1] // 3
    return pl.pallas_call(
        split_sums_body,
        out_shape=[jax.ShapeDtypeStruct((rows, width), f32), jax.ShapeDtypeStruct((rows, width), f32),
                   jax.ShapeDtypeStruct((width, rows), f32)],
        compiler_params=limits(56),
        cost_estimate=cost(2),
        name="split_sums",
    )(summed)


def shards(
    scan_input,
    gate_input,
    input_mix,
    output_mix,
    step_size,
    decay_rate,
    skip_scale,
    norm_gain,
    entry_state,
    out_weight,
    block_mid,
    expert_gain,
    expert_choice,
    route_weight,
    gate_proj,
    up_proj,
    down_proj,
    out_grad,
):
    channels = scan_input.shape[1]
    states = input_mix.shape[1]
    experts = lax.axis_size(EXP)
    ranges = lax.axis_size("seq")
    tokens = block_mid.shape[0]
    capacity = 4 * tokens // experts
    place = jnp.stack([lax.axis_index(axis) for axis in ("exp_0", "exp_1", "seq")]).astype(jnp.int32)
    rate, skip, gain = decay_rate[None], skip_scale[None], norm_gain[None]

    mid_values = block_mid.astype(f32)
    mid_scale = lax.rsqrt(jnp.mean(mid_values * mid_values, axis=1, keepdims=True) + norm_eps)
    tokens_out = payload(block_mid, expert_gain[None], expert_choice.T, route_weight.T)
    near = (shifted(tokens_out, "exp_0", 1), shifted(tokens_out, "exp_0", -1))

    y, normed, begin = scan_forward(
        scan_input, gate_input, input_mix, output_mix, step_size, rate, skip, gain,
        entry_state.reshape(channels, states),
    )
    near, y, grads_out = lax.optimization_barrier((near, y, out_grad))
    in_pieces = ring_rest(tokens_out, *near)
    grads_near = (shifted(grads_out, "exp_0", 1), shifted(grads_out, "exp_0", -1))

    gate_matrix, up_matrix, down_matrix = gate_proj[0], up_proj[0], down_proj[0]
    rows_in, share = collect(place, in_pieces, capacity)
    grads_near, rows_in = lax.optimization_barrier((grads_near, rows_in))
    grad_pieces = ring_rest(grads_out, *grads_near)
    gate_pre = dot(rows_in, gate_matrix)
    up_pre = dot(rows_in, up_matrix)
    grad_pieces, up_pre = lax.optimization_barrier((grad_pieces, up_pre))
    rows_grad = collect_scaled(share, grad_pieces, capacity)
    hidden_back = dot(rows_grad, down_matrix, NT)
    gate_act, gate_slope = silu_parts(gate_pre)
    hidden = (gate_act * up_pre).astype(bf16)
    gate_back = (hidden_back * up_pre * gate_slope).astype(bf16)
    up_back = (hidden_back * gate_act).astype(bf16)
    partials = row_partials(rows_in, rows_grad, gate_back, up_back, hidden)
    gate_back, up_back, partials = lax.optimization_barrier((gate_back, up_back, partials))
    rows_back = dot(gate_back, gate_matrix, NT) + dot(up_back, up_matrix, NT)
    parts = deliver(share, rows_back.astype(bf16))
    summed = lax.psum_scatter(partials, "seq", scatter_dimension=0, tiled=True)

    weighted_back = returned_sum(parts) * expert_gain
    mid_grad = (
        out_grad.astype(f32)
        + mid_scale * weighted_back
        - mid_values * mid_scale**3 * jnp.mean(mid_values * weighted_back, axis=1, keepdims=True)
    ).astype(bf16)
    out_back, gate_grad, end, joined, shard_rows = scan_backward(
        place, ring_pieces(mid_grad), out_weight, y, gate_input, output_mix, step_size, rate, gain
    )
    incoming = incoming_adjoint(joined)
    sent = out_partials(normed, shard_rows, ranges)
    out_parts = lax.all_to_all(sent, "seq", 0, 0, tiled=True)
    inner, in_part, out_mix_grad, log_part = scan_pairs(
        scan_input, out_back, input_mix, output_mix, step_size, rate, begin
    )
    input_grad, in_mix_grad, step_grad = scan_finish(
        scan_input, out_back, inner, input_mix, step_size, rate, skip, begin, end,
        in_part, log_part, incoming,
    )
    gate_sum, up_sum, down_sum = split_sums(summed)
    return (
        mid_grad,
        input_grad,
        gate_grad,
        in_mix_grad,
        out_mix_grad,
        step_grad,
        jnp.sum(out_parts.astype(f32), axis=0),
        gate_sum[None],
        up_sum[None],
        down_sum[None],
    )


def solution(mesh):
    split = Mesh(mesh.devices.reshape(mesh.shape["seq"], 4, 2), ("seq", "exp_0", "exp_1"))
    placed = (
        P("seq", EXP),
        P("seq", EXP),
        P(EXP, None, "seq"),
        P(EXP, None, "seq"),
        P(EXP, "seq"),
        P(EXP),
        P(EXP),
        P(EXP),
        P("seq", EXP, None, None),
        P(EXP, None),
        P(SEQ_EXP, None),
        P(),
        P(SEQ_EXP, None),
        P(SEQ_EXP, None),
        P(EXP, None, None),
        P(EXP, None, None),
        P(EXP, None, None),
        P(SEQ_EXP, None),
    )

    return jax.shard_map(
        shards,
        mesh=split,
        in_specs=placed,
        out_specs=(
            P(SEQ_EXP, None),
            P("seq", EXP),
            P("seq", EXP),
            P(EXP, None, "seq"),
            P(EXP, None, "seq"),
            P(EXP, "seq"),
            P(EXP, "seq"),
            P(EXP, "seq", None),
            P(EXP, "seq", None),
            P(EXP, None, "seq"),
        ),
        check_vma=False,
    )
```

```python
import jax
import jax.numpy as jnp
from jax import lax
from jax.experimental import pallas as pl
from jax.experimental.pallas import tpu as pltpu
from jax.sharding import Mesh
from jax.sharding import PartitionSpec as P

BLOCK = 256
EXP = ("exp_0", "exp_1")
SEQ_EXP = ("seq", "exp_0", "exp_1")
norm_eps = 1e-05
f32 = jnp.float32
bf16 = jnp.bfloat16


def dot(a, b, dims=((1,), (0,)), precision=None):
    return lax.dot_general(a, b, (dims, ((), ())), preferred_element_type=f32, precision=precision)


NT = ((1,), (1,))
TN = ((0,), (0,))


def split_two(value):
    high = value.astype(bf16)
    return high, (value - high.astype(f32)).astype(bf16)


def head_of_channel(heads, channels):
    row = lax.broadcasted_iota(jnp.int32, (heads, channels), 0)
    col = lax.broadcasted_iota(jnp.int32, (heads, channels), 1)
    return (col // (channels // heads) == row).astype(bf16)


def spread(per_head, owner):
    high, low = split_two(per_head)
    return dot(high, owner, TN) + dot(low, owner, TN)


def head_sums(owner, value):
    high, low = split_two(value)
    return dot(owner, high, NT) + dot(owner, low, NT)


def as_column(row):
    size = row.shape[1]
    same = lax.broadcasted_iota(jnp.int32, (size, size), 0) == lax.broadcasted_iota(jnp.int32, (size, size), 1)
    return jnp.sum(jnp.where(same, row, 0.0), axis=1, keepdims=True)


def in_hbm(shape, kind):
    return pltpu.HBM(shape, kind)


def limits(mib):
    return pltpu.CompilerParams(vmem_limit_bytes=mib << 20)


def cost(micros):
    return pl.CostEstimate(flops=int(micros * 9e8), transcendentals=0, bytes_accessed=int(micros * 2e6))


def head_row(owner, column):
    return jnp.sum(owner.astype(f32) * column, axis=0, keepdims=True)


def triangle_sums(rows, triangle):
    count = rows.shape[0]
    high, rest = rows.astype(bf16), rows - rows.astype(bf16).astype(f32)
    middle, low = split_two(rest)
    three = dot(jnp.concatenate([high.astype(f32), middle.astype(f32), low.astype(f32)], axis=0).astype(bf16),
                triangle.astype(bf16))
    return three[:count] + three[count : 2 * count] + three[2 * count :]


def log_cumulative(step, rate):
    tokens = step.shape[1]
    row = lax.broadcasted_iota(jnp.int32, (tokens, tokens), 0)
    col = lax.broadcasted_iota(jnp.int32, (tokens, tokens), 1)
    return triangle_sums(-step * rate, (row <= col).astype(f32))


def silu_parts(values):
    sigmoid = 1.0 / (1.0 + jnp.exp(-values))
    return values * sigmoid, sigmoid * (1.0 + values * (1.0 - sigmoid))


def forward_body(x_ref, z_ref, b_ref, c_ref, step_ref, rate_ref, skip_ref, gain_ref, entry_ref,
                 y_ref, normed_ref, begin_ref, state_ref):
    heads, tokens = step_ref.shape
    channels = x_ref.shape[1]
    width = channels // heads

    @pl.when(pl.program_id(0) == 0)
    def _():
        state_ref[...] = entry_ref[...].T

    owner = head_of_channel(heads, channels)
    x = x_ref[...].astype(f32)
    step = step_ref[...]
    log_cum = log_cumulative(step, as_column(rate_ref[...]))
    log_col = log_cum.T
    mix_in, mix_out = b_ref[...], c_ref[...]
    stepped = x * spread(step, owner)
    stepped_bf = stepped.astype(bf16)
    mix_dot = dot(mix_out, mix_in, TN)
    row = lax.broadcasted_iota(jnp.int32, (tokens, tokens), 0)
    col = lax.broadcasted_iota(jnp.int32, (tokens, tokens), 1)
    lower = row >= col
    parts = []
    for h in range(heads):
        gaps = log_col[:, h : h + 1] - log_cum[h : h + 1, :]
        kernel = (jnp.exp(jnp.where(lower, gaps, -1e30)) * mix_dot).astype(bf16)
        parts.append(dot(kernel, stepped_bf[:, h * width : (h + 1) * width]))
    state = state_ref[...]
    begin_ref[...] = state
    from_state = dot(mix_out.astype(f32), state, TN) * spread(jnp.exp(log_cum), owner)
    y = jnp.concatenate(parts, axis=1) + from_state + head_row(owner, as_column(skip_ref[...])) * x
    y_ref[...] = y
    last = log_cum[:, tokens - 1 :]
    ended = (stepped * spread(jnp.exp(last - log_cum), owner)).astype(bf16)
    state_ref[...] = head_row(owner, jnp.exp(last)) * state + dot(mix_in, ended)
    gate_act, _ = silu_parts(z_ref[...].astype(f32))
    gated = y * gate_act
    scale = lax.rsqrt(jnp.mean(gated * gated, axis=1, keepdims=True) + norm_eps)
    normed_ref[...] = (gated * scale * gain_ref[...]).astype(bf16)


def squeezed(*shape):
    return (pl.Squeezed(), *shape)


def scan_forward(x, z, mix_in, mix_out, step, rate, skip, gain, entry):
    length, channels = x.shape
    heads = step.shape[0]
    states = mix_in.shape[1]
    blocks = length // BLOCK
    whole = lambda shape: pl.BlockSpec(shape, lambda b: (0,) * len(shape))
    rows = pl.BlockSpec((BLOCK, channels), lambda b: (b, 0))
    mix = pl.BlockSpec(squeezed(states, BLOCK), lambda b: (0, 0, b))
    return pl.pallas_call(
        forward_body,
        grid=(blocks,),
        in_specs=[rows, rows, mix, mix, pl.BlockSpec((heads, BLOCK), lambda b: (0, b)),
                  whole((1, heads)), whole((1, heads)), whole((1, channels)), whole((channels, states))],
        out_specs=[rows, rows, pl.BlockSpec(squeezed(states, channels), lambda b: (b, 0, 0))],
        out_shape=[in_hbm((length, channels), f32),
                   in_hbm((length, channels), bf16),
                   in_hbm((blocks, states, channels), f32)],
        scratch_shapes=[pltpu.VMEM((states, channels), f32)],
        compiler_params=limits(24),
        cost_estimate=cost(9),
        name="scan_forward",
    )(x, z, mix_in, mix_out, step, rate, skip, gain, entry)


def backward_body(place_ref, *refs):
    pieces = refs[:14]
    (weight_ref, y_ref, z_ref, c_ref, step_ref, rate_ref, gain_ref,
     out_back_ref, gate_grad_ref, end_ref, joined_ref, rows_ref, state_ref, decay_ref, all_ref) = refs[14:]
    heads, tokens = step_ref.shape
    channels = y_ref.shape[1]
    states = state_ref.shape[0]

    @pl.when(pl.program_id(0) == 0)
    def _():
        state_ref[...] = jnp.zeros_like(state_ref)
        decay_ref[...] = jnp.ones_like(decay_ref)
        count = pieces[0].shape[0]
        half = count // 2
        for side in range(2):
            for turn in range(7):
                start = chunk_index(place_ref, side * 4 + (turn + 1) // 2) * count
                start = start + (half if turn in (2, 4, 6) else 0)
                piece = pieces[side * 7 + turn]
                all_ref[pl.ds(pl.multiple_of(start, half), piece.shape[0]), :] = piece[...]

    owner = head_of_channel(heads, channels)
    log_cum = log_cumulative(step_ref[...], as_column(rate_ref[...]))
    block = pl.num_programs(0) - 1 - pl.program_id(0)
    rows = all_ref[pl.ds(pl.multiple_of(block * tokens, tokens), tokens), :]
    rows_ref[...] = rows
    projected = dot(rows, weight_ref[...], NT)
    y = y_ref[...]
    gate_act, gate_slope = silu_parts(z_ref[...].astype(f32))
    gated = y * gate_act
    scale = lax.rsqrt(jnp.mean(gated * gated, axis=1, keepdims=True) + norm_eps)
    scaled = projected * gain_ref[...]
    inner = jnp.mean(gated * scaled, axis=1, keepdims=True)
    gated_back = scale * scaled - gated * (scale * scale * scale * inner)
    out_back = gated_back * gate_act
    gate_grad_ref[...] = (gated_back * y * gate_slope).astype(bf16)
    out_back_ref[...] = out_back
    state = state_ref[...]
    end_ref[...] = state
    decayed = (out_back * spread(jnp.exp(log_cum), owner)).astype(bf16)
    block_decay = head_row(owner, jnp.exp(log_cum[:, tokens - 1 :]))
    state = block_decay * state + dot(c_ref[...], decayed)
    decay = block_decay * decay_ref[...]
    state_ref[...] = state
    decay_ref[...] = decay
    joined_ref[:states, :] = state.astype(bf16)
    joined_ref[states:, :] = decay.astype(bf16)


def scan_backward(place, pieces, weight, y, z, mix_out, step, rate, gain):
    length, channels = y.shape
    heads = step.shape[0]
    states = mix_out.shape[1]
    blocks = length // BLOCK
    last = blocks - 1
    width = weight.shape[1]
    whole = lambda shape: pl.BlockSpec(shape, lambda b, place: (0,) * len(shape))
    rows = pl.BlockSpec((BLOCK, channels), lambda b, place: (last - b, 0))
    mix = pl.BlockSpec(squeezed(states, BLOCK), lambda b, place: (0, 0, last - b))
    return pl.pallas_call(
        backward_body,
        grid_spec=pltpu.PrefetchScalarGridSpec(
            num_scalar_prefetch=1,
            grid=(blocks,),
            in_specs=[whole(piece.shape) for piece in pieces] + [
                whole(weight.shape), rows, rows, mix,
                pl.BlockSpec((heads, BLOCK), lambda b, place: (0, last - b)),
                whole((1, heads)), whole((1, channels))],
            out_specs=[rows, rows, pl.BlockSpec(squeezed(states, channels), lambda b, place: (last - b, 0, 0)),
                       whole((states + 1, channels)),
                       pl.BlockSpec((BLOCK, width), lambda b, place: (last - b, 0))],
            scratch_shapes=[pltpu.VMEM((states, channels), f32), pltpu.VMEM((1, channels), f32),
                            pltpu.VMEM((length, width), bf16)],
        ),
        out_shape=[in_hbm((length, channels), f32),
                   in_hbm((length, channels), bf16),
                   in_hbm((blocks, states, channels), f32),
                   in_hbm((states + 1, channels), bf16),
                   in_hbm((length, width), bf16)],
        compiler_params=limits(56),
        cost_estimate=cost(9),
        name="scan_backward",
    )(place, *pieces, weight, y, z, mix_out, step, rate, gain)


def pairs_body(x_ref, ob_ref, b_ref, c_ref, step_ref, rate_ref, begin_ref,
               adj_ref, in_ref, out_ref, log_ref):
    heads, tokens = step_ref.shape
    channels = x_ref.shape[1]
    width = channels // heads
    owner = head_of_channel(heads, channels)
    step = step_ref[...]
    log_cum = log_cumulative(step, as_column(rate_ref[...]))
    log_col = log_cum.T
    mix_in, mix_out = b_ref[...], c_ref[...]
    out_back = ob_ref[...]
    out_back_bf = out_back.astype(bf16)
    stepped = (x_ref[...].astype(f32) * spread(step, owner)).astype(bf16)
    mix_dot = dot(mix_in, mix_out, TN)
    row = lax.broadcasted_iota(jnp.int32, (tokens, tokens), 0)
    col = lax.broadcasted_iota(jnp.int32, (tokens, tokens), 1)
    upper = row <= col
    group_pair = jnp.zeros((tokens, tokens), f32)
    parts, later, earlier = [], [], []
    for h in range(heads):
        gaps = log_cum[h : h + 1, :] - log_col[:, h : h + 1]
        decay = jnp.exp(jnp.where(upper, gaps, -1e30))
        mine = slice(h * width, (h + 1) * width)
        weighted = decay * dot(stepped[:, mine], out_back_bf[:, mine], NT)
        group_pair = group_pair + weighted
        terms = weighted * mix_dot
        later.append(jnp.sum(terms, axis=0, keepdims=True))
        earlier.append(jnp.sum(terms, axis=1, keepdims=True))
        parts.append(dot((decay * mix_dot).astype(bf16), out_back_bf[:, mine]))
    adj_ref[...] = jnp.concatenate(parts, axis=1)
    begin = begin_ref[...]
    decayed = out_back * spread(jnp.exp(log_cum), owner)
    pair_bf = group_pair.astype(bf16)
    in_ref[...] = dot(mix_out, pair_bf, NT)
    out_ref[...] = dot(mix_in, pair_bf) + dot(begin.astype(bf16), decayed.astype(bf16), NT)
    from_state = dot(mix_out.astype(f32), begin, TN)
    net = jnp.concatenate(later, axis=0) - jnp.concatenate(earlier, axis=1).T
    net = net + head_sums(owner, decayed * from_state)
    log_ref[...] = triangle_sums(net, (row >= col).astype(f32))


def scan_pairs(x, out_back, mix_in, mix_out, step, rate, begin):
    length, channels = x.shape
    heads = step.shape[0]
    states = mix_out.shape[1]
    blocks = length // BLOCK
    whole = lambda shape: pl.BlockSpec(shape, lambda b: (0,) * len(shape))
    rows = pl.BlockSpec((BLOCK, channels), lambda b: (b, 0))
    mix = pl.BlockSpec(squeezed(states, BLOCK), lambda b: (0, 0, b))
    line = pl.BlockSpec((heads, BLOCK), lambda b: (0, b))
    return pl.pallas_call(
        pairs_body,
        grid=(blocks,),
        in_specs=[rows, rows, mix, mix, line, whole((1, heads)),
                  pl.BlockSpec(squeezed(states, channels), lambda b: (b, 0, 0))],
        out_specs=[rows, mix, mix, line],
        out_shape=[in_hbm((length, channels), f32),
                   in_hbm((1, states, length), f32),
                   in_hbm((1, states, length), f32),
                   in_hbm((heads, length), f32)],
        compiler_params=limits(56),
        cost_estimate=cost(11),
        name="scan_pairs",
    )(x, out_back, mix_in, mix_out, step, rate, begin)


def finish_body(x_ref, ob_ref, adj_ref, b_ref, step_ref, rate_ref, skip_ref, begin_ref, end_ref,
                in_part_ref, log_part_ref, incoming_ref,
                grad_ref, in_ref, step_grad_ref, carried_ref):
    heads, tokens = step_ref.shape
    channels = x_ref.shape[1]

    @pl.when(pl.program_id(0) == 0)
    def _():
        carried_ref[...] = incoming_ref[...]

    owner = head_of_channel(heads, channels)
    x = x_ref[...].astype(f32)
    step = step_ref[...]
    rate = as_column(rate_ref[...])
    log_cum = log_cumulative(step, rate)
    last = log_cum[:, tokens - 1 :]
    carried = carried_ref[...]
    end = end_ref[...] + carried
    mix_in = b_ref[...]
    end_decay = spread(jnp.exp(last - log_cum), owner)
    stepped = spread(step, owner)
    end_back = dot(mix_in.astype(f32), end, TN) * end_decay
    adjoint = adj_ref[...] + end_back
    grad_ref[...] = (head_row(owner, as_column(skip_ref[...])) * ob_ref[...] + stepped * adjoint).astype(bf16)
    in_ref[...] = in_part_ref[...] + dot(end.astype(bf16), (stepped * end_decay * x).astype(bf16), NT)
    end_term = step * head_sums(owner, x * end_back)
    row = lax.broadcasted_iota(jnp.int32, (tokens, tokens), 0)
    col = lax.broadcasted_iota(jnp.int32, (tokens, tokens), 1)
    block_decay = jnp.exp(last)
    both = jnp.sum(end * begin_ref[...], axis=0, keepdims=True)
    whole_term = block_decay * jnp.sum(owner.astype(f32) * both, axis=1, keepdims=True)
    log_grad = log_part_ref[...] + triangle_sums(end_term, (row < col).astype(f32)) + whole_term
    step_grad_ref[...] = head_sums(owner, x * adjoint) - rate * log_grad
    carried_ref[...] = head_row(owner, block_decay) * carried


def scan_finish(x, out_back, adjoint, mix_in, step, rate, skip, begin, end, in_part, log_part, incoming):
    length, channels = x.shape
    heads = step.shape[0]
    states = mix_in.shape[1]
    blocks = length // BLOCK
    last = blocks - 1
    whole = lambda shape: pl.BlockSpec(shape, lambda b: (0,) * len(shape))
    rows = pl.BlockSpec((BLOCK, channels), lambda b: (last - b, 0))
    mix = pl.BlockSpec(squeezed(states, BLOCK), lambda b: (0, 0, last - b))
    line = pl.BlockSpec((heads, BLOCK), lambda b: (0, last - b))
    state = pl.BlockSpec(squeezed(states, channels), lambda b: (last - b, 0, 0))
    return pl.pallas_call(
        finish_body,
        grid=(blocks,),
        in_specs=[rows, rows, rows, mix, line, whole((1, heads)), whole((1, heads)), state, state,
                  mix, line, whole(incoming.shape)],
        out_specs=[rows, mix, line],
        scratch_shapes=[pltpu.VMEM((states, channels), f32)],
        out_shape=[in_hbm((length, channels), bf16),
                   in_hbm((1, states, length), f32),
                   in_hbm((heads, length), f32)],
        compiler_params=limits(56),
        cost_estimate=cost(9),
        name="scan_finish",
    )(x, out_back, adjoint, mix_in, step, rate, skip, begin, end, in_part, log_part, incoming)


CHUNKS = 8
OFFSETS = (0, -1, 1, 2)


def shifted(value, axis, by):
    size = lax.axis_size(axis)
    return lax.ppermute(value, axis, [(k, (k + by) % size) for k in range(size)])


def swapped(value):
    return shifted(value, "exp_1", 1)


def ring_rest(rows, right, left):
    half = rows.shape[0] // 2
    ahead = shifted(right[:half], "exp_0", 1)
    behind = shifted(left[half:], "exp_0", -1)
    local = [rows, right, left, ahead, behind]
    return local + [swapped(piece) for piece in local]


def half_ring(rows):
    half = rows.shape[0] // 2
    low, high = rows[:half], rows[half:]
    right_low, left_high = shifted(low, "exp_0", 1), shifted(high, "exp_0", -1)
    right_high, left_low = shifted(high, "exp_0", 1), shifted(low, "exp_0", -1)
    ahead, behind = shifted(right_low, "exp_0", 1), shifted(left_high, "exp_0", -1)
    local = [rows, right_low, right_high, left_low, left_high, ahead, behind]
    return local + [swapped(piece) for piece in local]


def chunk_index(place_ref, slot):
    chip, core = place_ref[0], place_ref[1]
    return (chip + OFFSETS[slot % 4] + 4) % 4 * 2 + (core + slot // 4) % 2


def chunk_values(refs, slot):
    side, turn = slot // 4 * 5, slot % 4
    if turn < 3:
        return refs[side + turn][...]
    return jnp.concatenate([refs[side + 3][...], refs[side + 4][...]], axis=0)


PARTS = 3
EXTRA = 128


def payload_body(mid_ref, gain_ref, choice_ref, weight_ref, out_ref):
    width = mid_ref.shape[1]
    mid = mid_ref[...].astype(f32)
    scale = lax.rsqrt(jnp.mean(mid * mid, axis=1, keepdims=True) + norm_eps)
    out_ref[:, :width] = (mid * scale * gain_ref[...]).astype(bf16)
    tokens = choice_ref.shape[1]
    lines = jnp.concatenate(
        [choice_ref[...].astype(f32), weight_ref[...], jnp.zeros((4, tokens), f32)], axis=0
    ).T
    lane = lax.broadcasted_iota(jnp.int32, (tokens, EXTRA), 1)
    owner, part = (lane // PARTS).astype(f32), lane % PARTS
    held = jnp.zeros((tokens, EXTRA), f32)
    for k in range(2):
        share = lines[:, 2 + k : 3 + k]
        high = share.astype(bf16).astype(f32)
        middle = (share - high).astype(bf16).astype(f32)
        low = share - high - middle
        value = jnp.where(part == 0, high, jnp.where(part == 1, middle, low))
        held = held + jnp.where(owner == lines[:, k : k + 1], value, 0.0)
    out_ref[:, width:] = held.astype(bf16)


def payload(mid, gain, choice, weight):
    tokens, width = mid.shape
    return pl.pallas_call(
        payload_body,
        out_shape=jax.ShapeDtypeStruct((tokens, width + EXTRA), bf16),
        compiler_params=limits(56),
        cost_estimate=cost(2),
        name="payload",
    )(mid, gain, choice, weight)


def slots_of(share, capacity):
    tokens = share.shape[1]
    hit = share > 0
    row = lax.broadcasted_iota(jnp.int32, (tokens, tokens), 0)
    col = lax.broadcasted_iota(jnp.int32, (tokens, tokens), 1)
    before = dot(hit.astype(f32).astype(bf16), (row < col).astype(f32).astype(bf16))
    rank = jnp.where(hit, before, -1.0)
    place = lax.broadcasted_iota(jnp.int32, (capacity, tokens), 0).astype(f32)
    return [place == rank[slot : slot + 1] for slot in range(share.shape[0])]


def collect_body(place_ref, *refs):
    pieces, extras, out_ref, share_ref = refs[:10], refs[10:20], refs[20], refs[21]
    capacity = out_ref.shape[0] // CHUNKS
    lane = lax.broadcasted_iota(jnp.int32, (8, EXTRA), 1)
    mine = (lane // PARTS == place_ref[0] * 2 + place_ref[1]).astype(f32).astype(bf16)
    share = jnp.concatenate(
        [dot(mine, chunk_values(extras, slot), NT)[:1] for slot in range(CHUNKS)], axis=0
    )
    share_ref[...] = share
    for slot, chosen in enumerate(slots_of(share, capacity)):
        rows = dot(chosen.astype(f32).astype(bf16), chunk_values(pieces, slot))
        out_ref[slot * capacity : (slot + 1) * capacity, :] = rows.astype(bf16)


TILES = 4


def collect(place, pieces, capacity):
    width = pieces[0].shape[1] - EXTRA
    tokens = pieces[0].shape[0]
    tile = width // TILES
    cut = lambda rows: pl.BlockSpec((rows, tile), lambda i, place: (0, i))
    extra = lambda rows: pl.BlockSpec((rows, EXTRA), lambda i, place: (0, width // EXTRA))
    return pl.pallas_call(
        collect_body,
        grid_spec=pltpu.PrefetchScalarGridSpec(
            num_scalar_prefetch=1,
            grid=(TILES,),
            in_specs=[cut(leaf.shape[0]) for leaf in pieces] + [extra(leaf.shape[0]) for leaf in pieces],
            out_specs=[cut(CHUNKS * capacity), pl.BlockSpec((CHUNKS, tokens), lambda i, place: (0, 0))],
        ),
        out_shape=[jax.ShapeDtypeStruct((CHUNKS * capacity, width), bf16),
                   jax.ShapeDtypeStruct((CHUNKS, tokens), f32)],
        compiler_params=limits(16),
        cost_estimate=cost(4),
        name="collect",
    )(place, *pieces, *pieces)


def collect_scaled_body(share_ref, *refs):
    pieces, out_ref = refs[:10], refs[10]
    capacity = out_ref.shape[0] // CHUNKS
    share = share_ref[...]
    for slot, chosen in enumerate(slots_of(share, capacity)):
        rows = dot(chosen.astype(f32).astype(bf16), chunk_values(pieces, slot))
        weight = jnp.sum(jnp.where(chosen, share[slot : slot + 1], 0.0), axis=1, keepdims=True)
        out_ref[slot * capacity : (slot + 1) * capacity, :] = (rows * weight).astype(bf16)


def column_call(body, share, arrays, out_shape, micros):
    tile = arrays[0].shape[1] // TILES
    cut = lambda leaf: pl.BlockSpec((leaf.shape[0], tile), lambda i: (0, i))
    return pl.pallas_call(
        body,
        grid=(TILES,),
        in_specs=[pl.BlockSpec(share.shape, lambda i: (0, 0))] + [cut(leaf) for leaf in arrays],
        out_specs=jax.tree.map(cut, out_shape),
        out_shape=out_shape,
        compiler_params=limits(16),
        cost_estimate=cost(micros),
    )(share, *arrays)


def collect_scaled(share, pieces, capacity):
    shape = jax.ShapeDtypeStruct((CHUNKS * capacity, pieces[0].shape[1]), bf16)
    return column_call(collect_scaled_body, share, pieces, shape, 4)


def deliver_body(share_ref, rows_ref, *outs):
    capacity = rows_ref.shape[0] // CHUNKS
    for slot, chosen in enumerate(slots_of(share_ref[...], capacity)):
        rows = rows_ref[slot * capacity : (slot + 1) * capacity, :]
        outs[slot][...] = dot(chosen.astype(f32).astype(bf16), rows, TN).astype(bf16)


def deliver(share, rows):
    shape = jax.ShapeDtypeStruct((share.shape[1], rows.shape[1]), bf16)
    return column_call(deliver_body, share, [rows], [shape] * CHUNKS, 3)


def returned_sum(parts):
    here = [part + swapped(other) for part, other in zip(parts[:4], parts[4:])]
    mine, behind, ahead, across = here
    half = mine.shape[0] // 2
    first = shifted(jnp.concatenate([across[:half], ahead[half:]], axis=0), "exp_0", 1)
    second = shifted(jnp.concatenate([behind[:half], across[half:]], axis=0), "exp_0", -1)
    left = shifted(ahead[:half] + first[:half], "exp_0", 1)
    right = shifted(behind[half:] + second[half:], "exp_0", -1)
    wide = lambda part: part.astype(f32)
    return wide(mine) + jnp.concatenate(
        [wide(left) + wide(second[:half]), wide(first[half:]) + wide(right)], axis=0
    )


def out_partials_body(left_ref, right_ref, out_ref, turned_ref):
    width = out_ref.shape[2]

    @pl.when(pl.program_id(0) == 0)
    def _():
        turned_ref[...] = left_ref[...].T

    product = dot(turned_ref[...], right_ref[...]).astype(bf16)
    for k in range(out_ref.shape[0]):
        out_ref[k] = product[:, k * width : (k + 1) * width]


def out_partials(left, right, pieces):
    rows, height = left.shape
    width = right.shape[1] // pieces
    return pl.pallas_call(
        out_partials_body,
        grid=(pieces // 4,),
        in_specs=[pl.BlockSpec((rows, height), lambda i: (0, 0)),
                  pl.BlockSpec((rows, 4 * width), lambda i: (0, i))],
        out_specs=pl.BlockSpec((4, height, width), lambda i: (i, 0, 0)),
        out_shape=in_hbm((pieces, height, width), bf16),
        scratch_shapes=[pltpu.VMEM((height, rows), bf16)],
        compiler_params=limits(56),
        cost_estimate=cost(5),
        name="out_partials",
    )(left, right)


def row_partials_body(in_ref, grad_ref, gate_ref, up_ref, hidden_ref, out_ref):
    width = gate_ref.shape[1]
    turned = in_ref[...].T
    out_ref[:, :width] = dot(turned, gate_ref[...]).astype(bf16)
    out_ref[:, width : 2 * width] = dot(turned, up_ref[...]).astype(bf16)
    out_ref[:, 2 * width :] = dot(grad_ref[...].T, hidden_ref[...]).astype(bf16)


def row_partials(rows_in, rows_grad, gate, up, hidden):
    rows, height = rows_in.shape
    width = gate.shape[1]
    tile = 512
    cut = pl.BlockSpec((rows, tile), lambda i: (0, i))
    whole = pl.BlockSpec((rows, width), lambda i: (0, 0))
    return pl.pallas_call(
        row_partials_body,
        grid=(height // tile,),
        in_specs=[cut, cut, whole, whole, whole],
        out_specs=pl.BlockSpec((tile, 3 * width), lambda i: (i, 0)),
        out_shape=in_hbm((height, 3 * width), bf16),
        compiler_params=limits(24),
        cost_estimate=cost(9),
        name="row_partials",
    )(rows_in, rows_grad, gate, up, hidden)


def row_of(joined):
    joined = joined.astype(f32)
    return joined[:-1], joined[-1:]


def incoming_adjoint(joined):
    size = lax.axis_size("seq")
    side = 4
    mine = lax.axis_index("seq")
    column, row = mine % side, mine // side

    def from_column(value, by):
        return lax.ppermute(
            value, "seq", [(k // side * side + (k + by) % side, k) for k in range(size)])

    def from_row(value, by):
        return lax.ppermute(value, "seq", [((k + by * side) % size, k) for k in range(size)])

    adjoint, decay = row_of(joined)
    others = [row_of(from_column(joined, by)) for by in range(1, side)]
    after, reach = jnp.zeros_like(adjoint), jnp.ones_like(decay)
    for by in range(side - 1, 0, -1):
        there, fade = others[by - 1]
        valid = column + by < side
        after = jnp.where(valid, there + fade * after, after)
        reach = jnp.where(valid, fade * reach, reach)
    total, whole = adjoint + decay * after, decay
    for by in range(side - 1, 0, -1):
        there, fade = others[by - 1]
        total = jnp.where(column + by >= side, there + fade * total, total)
        whole = whole * fade
    sent = jnp.concatenate([total, whole], axis=0).astype(bf16)
    rows = [from_row(sent, by) for by in range(1, size // side)]
    rows = [row_of(value) for value in rows]
    beyond = jnp.zeros_like(adjoint)
    for by in range(size // side - 1, 0, -1):
        there, fade = rows[by - 1]
        beyond = jnp.where(row + by < size // side, there + fade * beyond, beyond)
    return after + reach * beyond


def split_sums_body(sum_ref, gate_ref, up_ref, down_ref):
    width = gate_ref.shape[1]
    gate_ref[...] = sum_ref[:, :width].astype(f32)
    up_ref[...] = sum_ref[:, width : 2 * width].astype(f32)
    down_ref[...] = sum_ref[:, 2 * width :].astype(f32).T


def split_sums(summed):
    rows, width = summed.shape[0], summed.shape[1] // 3
    return pl.pallas_call(
        split_sums_body,
        out_shape=[jax.ShapeDtypeStruct((rows, width), f32), jax.ShapeDtypeStruct((rows, width), f32),
                   jax.ShapeDtypeStruct((width, rows), f32)],
        compiler_params=limits(56),
        cost_estimate=cost(2),
        name="split_sums",
    )(summed)


def shards(
    scan_input,
    gate_input,
    input_mix,
    output_mix,
    step_size,
    decay_rate,
    skip_scale,
    norm_gain,
    entry_state,
    out_weight,
    block_mid,
    expert_gain,
    expert_choice,
    route_weight,
    gate_proj,
    up_proj,
    down_proj,
    out_grad,
):
    channels = scan_input.shape[1]
    states = input_mix.shape[1]
    experts = lax.axis_size(EXP)
    ranges = lax.axis_size("seq")
    tokens = block_mid.shape[0]
    capacity = 4 * tokens // experts
    place = jnp.stack([lax.axis_index(axis) for axis in ("exp_0", "exp_1", "seq")]).astype(jnp.int32)
    rate, skip, gain = decay_rate[None], skip_scale[None], norm_gain[None]

    mid_values = block_mid.astype(f32)
    mid_scale = lax.rsqrt(jnp.mean(mid_values * mid_values, axis=1, keepdims=True) + norm_eps)
    tokens_out = payload(block_mid, expert_gain[None], expert_choice.T, route_weight.T)
    near = (shifted(tokens_out, "exp_0", 1), shifted(tokens_out, "exp_0", -1))

    y, normed, begin = scan_forward(
        scan_input, gate_input, input_mix, output_mix, step_size, rate, skip, gain,
        entry_state.reshape(channels, states),
    )
    near, y, grads_out = lax.optimization_barrier((near, y, out_grad))
    in_pieces = ring_rest(tokens_out, *near)
    grads_near = (shifted(grads_out, "exp_0", 1), shifted(grads_out, "exp_0", -1))

    gate_matrix, up_matrix, down_matrix = gate_proj[0], up_proj[0], down_proj[0]
    rows_in, share = collect(place, in_pieces, capacity)
    grads_near, rows_in = lax.optimization_barrier((grads_near, rows_in))
    grad_pieces = ring_rest(grads_out, *grads_near)
    gate_pre = dot(rows_in, gate_matrix)
    up_pre = dot(rows_in, up_matrix)
    grad_pieces, up_pre = lax.optimization_barrier((grad_pieces, up_pre))
    rows_grad = collect_scaled(share, grad_pieces, capacity)
    hidden_back = dot(rows_grad, down_matrix, NT)
    gate_act, gate_slope = silu_parts(gate_pre)
    hidden = (gate_act * up_pre).astype(bf16)
    gate_back = (hidden_back * up_pre * gate_slope).astype(bf16)
    up_back = (hidden_back * gate_act).astype(bf16)
    partials = row_partials(rows_in, rows_grad, gate_back, up_back, hidden)
    gate_back, up_back, partials = lax.optimization_barrier((gate_back, up_back, partials))
    rows_back = dot(gate_back, gate_matrix, NT) + dot(up_back, up_matrix, NT)
    parts = deliver(share, rows_back.astype(bf16))
    summed = lax.psum_scatter(partials, "seq", scatter_dimension=0, tiled=True)

    weighted_back = returned_sum(parts) * expert_gain
    mid_grad = (
        out_grad.astype(f32)
        + mid_scale * weighted_back
        - mid_values * mid_scale**3 * jnp.mean(mid_values * weighted_back, axis=1, keepdims=True)
    ).astype(bf16)
    out_back, gate_grad, end, joined, shard_rows = scan_backward(
        place, half_ring(mid_grad), out_weight, y, gate_input, output_mix, step_size, rate, gain
    )
    incoming = incoming_adjoint(joined)
    sent = out_partials(normed, shard_rows, ranges)
    out_parts = lax.all_to_all(sent, "seq", 0, 0, tiled=True)
    inner, in_part, out_mix_grad, log_part = scan_pairs(
        scan_input, out_back, input_mix, output_mix, step_size, rate, begin
    )
    input_grad, in_mix_grad, step_grad = scan_finish(
        scan_input, out_back, inner, input_mix, step_size, rate, skip, begin, end,
        in_part, log_part, incoming,
    )
    gate_sum, up_sum, down_sum = split_sums(summed)
    return (
        mid_grad,
        input_grad,
        gate_grad,
        in_mix_grad,
        out_mix_grad,
        step_grad,
        jnp.sum(out_parts.astype(f32), axis=0),
        gate_sum[None],
        up_sum[None],
        down_sum[None],
    )


def solution(mesh):
    split = Mesh(mesh.devices.reshape(mesh.shape["seq"], 4, 2), ("seq", "exp_0", "exp_1"))
    placed = (
        P("seq", EXP),
        P("seq", EXP),
        P(EXP, None, "seq"),
        P(EXP, None, "seq"),
        P(EXP, "seq"),
        P(EXP),
        P(EXP),
        P(EXP),
        P("seq", EXP, None, None),
        P(EXP, None),
        P(SEQ_EXP, None),
        P(),
        P(SEQ_EXP, None),
        P(SEQ_EXP, None),
        P(EXP, None, None),
        P(EXP, None, None),
        P(EXP, None, None),
        P(SEQ_EXP, None),
    )

    return jax.shard_map(
        shards,
        mesh=split,
        in_specs=placed,
        out_specs=(
            P(SEQ_EXP, None),
            P("seq", EXP),
            P("seq", EXP),
            P(EXP, None, "seq"),
            P(EXP, None, "seq"),
            P(EXP, "seq"),
            P(EXP, "seq"),
            P(EXP, "seq", None),
            P(EXP, "seq", None),
            P(EXP, None, "seq"),
        ),
        check_vma=False,
    )
```
